32 devices in a mesh: gz: 8 (over z, core), xy: 4 (over y, x).
Axes of the slice: x: 2, y: 2, z: 4, core: 2. Of those that a mesh axis runs over, the one named last changes fastest.
Arguments:
- slab_image: float32 [32, 128, 1024], P('gz', None, 'xy'), may hold values from 0 to 1
- width_taps: float32 [16, 5], replicated, may hold values from -2.5 to 2.5
- height_taps: float32 [16, 5], replicated, may hold values from -2.5 to 2.5
- depth_taps: float32 [16, 5], replicated, may hold values from -2.5 to 2.5
- fragment_ids: int32 [32, 128, 1024], P(None, 'gz', 'xy'), may hold values from 0 to 1023, as said below
- fragment_owner: int32 [32768, 1], P(('gz', 'xy')), may hold values from 0 to 3, as said below
- coarse_centroids: float32 [16, 1024], P(None, ('gz', 'xy')), may hold values from -24 to 24
- parent_map: int32 [4096], P(('gz', 'xy')), may hold values from 0 to 31
- fine_offsets: float32 [16, 4096], P(None, ('gz', 'xy')), may hold values from -2.5 to 2.5
Outputs:
- fragment_means: float32 [16, 32768], P(None, ('gz', 'xy'))
- centroids: float32 [16, 4096], P(None, ('gz', 'xy'))
The draws below stay inside these ranges and needn't reach their ends.
Inputs may be any that keep to these rules, and one draw needn't show every extreme that they name: `fragment_ids`: ids are local to a pencil block of 32 x 16 x 256 voxels; every id 0 to 1023 occurs in every block. `fragment_owner`: of the 1024 fragments of one pencil block at most 512 name the same owner; in each row along xy some owner takes exactly 512 from every block of that row.
All inputs are finite; a program needn't handle non-finite values.
Results may differ from the reference program's by a relative error of at most 0.00038.
Values may be sent and summed in bfloat16 or wider, within the bound.
A program may use at most 128 MiB of HBM per device.

```python
import jax
import jax.numpy as jnp
from jax import lax

CH = 16
TAPS = 5
YCOL = 16
XROW = 256
BZ = 4
BY = 4
BX = 8
KF_DEV = 128
KC_DEV = 32
ITERS = 3
NZ = 32
NY = 128
NX = 1024
FL = 1024
NF = 32768
CAP = 512
KF = 4096
KC = 1024
PSEUDO = 1024
N_GZ = 8
N_XY = 4


def fragment_volume(key):
    devices = N_GZ * N_XY
    bricks_y = YCOL // BY
    bricks_x = XROW // BX
    zpos = jnp.arange(NZ, dtype=jnp.int32)[:, None, None]
    ypos = jnp.arange(YCOL, dtype=jnp.int32)[None, :, None]
    xpos = jnp.arange(XROW, dtype=jnp.int32)[None, None, :]
    brick = zpos // BZ * (bricks_y * bricks_x) + ypos // BY * bricks_x + xpos // BX
    moved = zpos // BZ * (bricks_y * bricks_x) + ypos // BY * bricks_x + (xpos // BX + 1) % bricks_x
    inner = zpos % BZ + ypos % BY + xpos % BX
    flag = jax.random.randint(jax.random.fold_in(key, 21), (devices, NZ, YCOL, XROW), 0, 8) == 0
    flag = jnp.logical_and(flag, (inner > 0)[None])
    brick = jnp.where(flag, moved[None], brick[None])
    keys = jax.random.split(jax.random.fold_in(key, 22), devices)
    relabel = jax.vmap(lambda single: jax.random.permutation(single, FL))(keys).astype(jnp.int32)
    local = jnp.take_along_axis(relabel, brick.reshape(devices, -1), axis=1)
    return local.reshape(devices, NZ, YCOL, XROW)


def arrange(local):
    grid = local.reshape(N_GZ, N_XY, NZ, YCOL, XROW)
    grid = jnp.transpose(grid, (2, 0, 3, 1, 4))
    return grid.reshape(NZ, NY, NX)


def draw_fragment_ids(key, part):
    return arrange(fragment_volume(key)).astype(jnp.int32)


def draw_slab_image(key, part):
    local = fragment_volume(key)
    devices = N_GZ * N_XY
    levels = jax.random.uniform(jax.random.fold_in(key, 23), (devices, FL), minval=-1.0, maxval=1.0)
    level = jnp.take_along_axis(levels, local.reshape(devices, -1), axis=1).reshape(local.shape)
    noise = jax.random.uniform(jax.random.fold_in(key, 24), local.shape, minval=-1.0, maxval=1.0)
    values = 0.5 + 0.3 * level + 0.2 * noise
    return arrange(values).astype(jnp.float32)


def draw_fragment_owner(key, part):
    devices = N_GZ * N_XY
    heavy = jax.random.randint(jax.random.fold_in(key, 41), (N_GZ, 1), 0, N_XY)
    heavy = jnp.repeat(heavy, N_XY, axis=0)
    rows = jnp.arange(FL, dtype=jnp.int32)[None, :]
    spill = min(FL - CAP, CAP // 2)
    others = N_XY - 1
    random_part = jax.random.randint(jax.random.fold_in(key, 42), (devices, FL), 0, others)
    offset_start = jax.random.randint(jax.random.fold_in(key, 43), (devices, 1), 0, others)
    cycled = (rows - CAP - spill + offset_start) % others
    offset = jnp.where(rows < CAP + spill, random_part, cycled)
    owner = jnp.where(rows < CAP, heavy, (heavy + 1 + offset) % N_XY)
    keys = jax.random.split(jax.random.fold_in(key, 44), devices)
    shuffle = jax.vmap(lambda single: jax.random.permutation(single, FL))(keys)
    owner = jnp.take_along_axis(owner, shuffle, axis=1)
    return owner.reshape(devices * FL, 1).astype(jnp.int32)


def draw_coarse_centroids(key, part):
    base = jnp.clip(jax.random.normal(jax.random.fold_in(key, 51), (CH, KC)), -4.0, 4.0) * 0.6
    return base.astype(jnp.float32)


def plant(drawn, key, smallest, top_value):
    place = [jax.random.randint(jax.random.fold_in(key, axis), (), 0, length) for axis, length in enumerate(drawn.shape)]
    longest = drawn.shape.index(max(drawn.shape))
    beside = place[:longest] + [(place[longest] + 1) % drawn.shape[longest]] + place[longest + 1:]
    return drawn.at[tuple(place)].set(smallest).at[tuple(beside)].set(top_value)


def level_of(stream_key, dims, pieces, low, largest):
    level = 1.0
    for axis_at, shards_of in pieces:
        heights = jax.random.uniform(jax.random.fold_in(jax.random.fold_in(stream_key, 6), axis_at), (shards_of,), jnp.float32, low / len(pieces), largest / len(pieces))
        level = level * jnp.repeat(jnp.exp(heights), dims[axis_at] // shards_of).reshape((-1,) + (1,) * (len(dims) - 1 - axis_at))
    return level


def scatter_about(key, dims, width, reach, cuts=(), kind=jnp.bfloat16):
    level = level_of(key, dims, cuts, -0.22, 0.18) if cuts else 1.0
    values = jax.random.normal(key, dims, jnp.float32) * width * level
    return jnp.minimum(jnp.maximum(values, -reach), reach).astype(kind)


def setup_inputs(seed: int = 0) -> dict:
    key_of = jax.random.split(jax.random.key(seed), 10)
    return {
        "slab_image": draw_slab_image(jax.random.fold_in(key_of[9], 71), 0),
        "width_taps": scatter_about(key_of[1], (CH, TAPS), 0.5, 2.5, (), jnp.float32),
        "height_taps": scatter_about(key_of[2], (CH, TAPS), 0.5, 2.5, (), jnp.float32),
        "depth_taps": scatter_about(key_of[3], (CH, TAPS), 0.5, 2.5, (), jnp.float32),
        "fragment_ids": draw_fragment_ids(jax.random.fold_in(key_of[9], 71), 0),
        "fragment_owner": draw_fragment_owner(jax.random.fold_in(key_of[9], 71), 0),
        "coarse_centroids": draw_coarse_centroids(jax.random.fold_in(key_of[9], 71), 0),
        "parent_map": plant(jax.random.randint(key_of[7], (KF,), 0, KC_DEV), jax.random.fold_in(key_of[7], 1), 0, KC_DEV - 1).astype(jnp.int32),
        "fine_offsets": scatter_about(key_of[8], (CH, KF), 0.25, 2.5, ((1, 32),), jnp.float32),
    }


HIGH = lax.Precision.HIGHEST
sharpness = 2.0


def planar_channel(volume, width_tap, height_tap):
    half = TAPS // 2
    padded = jnp.pad(volume, ((0, 0), (half, half), (half, half)))
    rows = volume.shape[1]
    cols = volume.shape[2]
    across = width_tap[0] * padded[:, :, 0:cols]
    for tap_shift in range(1, TAPS):
        across = across + width_tap[tap_shift] * padded[:, :, tap_shift:tap_shift + cols]
    planar = height_tap[0] * across[:, 0:rows, :]
    for tap_shift in range(1, TAPS):
        planar = planar + height_tap[tap_shift] * across[:, tap_shift:tap_shift + rows, :]
    return planar.astype(jnp.bfloat16)


def soft_stats(frags, weight, cents, allowed):
    cross = lax.dot_general(frags, cents, (((0,), (0,)), ((), ())), precision=HIGH, preferred_element_type=jnp.float32)
    distance = jnp.sum(frags * frags, axis=0)[:, None] + jnp.sum(cents * cents, axis=0)[None, :] - 2.0 * cross
    scores = jnp.where(allowed, -sharpness * distance, -jnp.inf)
    top = jnp.max(scores, axis=1, keepdims=True)
    expo = jnp.exp(scores - top)
    resp = expo / jnp.sum(expo, axis=1, keepdims=True)
    numer = jnp.dot(frags * weight[None, :], resp, precision=HIGH, preferred_element_type=jnp.float32)
    denom = jnp.dot(weight[None, :], resp, precision=HIGH, preferred_element_type=jnp.float32)
    return numer, denom[0]


def reference(slab_image, width_taps, height_taps, depth_taps, fragment_ids, fragment_owner, coarse_centroids, parent_map, fine_offsets):
    half = TAPS // 2
    ypos = jnp.arange(NY, dtype=jnp.int32)[None, :, None] // YCOL
    xpos = jnp.arange(NX, dtype=jnp.int32)[None, None, :] // XROW
    labels = ((ypos * N_XY + xpos) * FL + fragment_ids).astype(jnp.int32)
    flat_labels = labels.reshape(-1)

    def channel_terms(taps):
        width_tap, height_tap, depth_tap = taps
        planar = planar_channel(slab_image, width_tap, height_tap)
        planar = lax.optimization_barrier(planar).astype(jnp.float32)
        padded = jnp.pad(planar, ((half, half), (0, 0), (0, 0)))
        response = depth_tap[0] * padded[0:NZ]
        for tap_shift in range(1, TAPS):
            response = response + depth_tap[tap_shift] * padded[tap_shift:tap_shift + NZ]
        feature = jnp.tanh(response).astype(jnp.bfloat16)
        feature = lax.optimization_barrier(feature).astype(jnp.float32)
        return jax.ops.segment_sum(feature.reshape(-1), flat_labels, num_segments=NF)

    feature_sum = lax.map(channel_terms, (width_taps, height_taps, depth_taps))
    voxel_count = jax.ops.segment_sum(jnp.ones(flat_labels.shape, jnp.float32), flat_labels, num_segments=NF)
    fragment_means = feature_sum / voxel_count[None, :]

    block = jnp.arange(KF, dtype=jnp.int32) // KF_DEV
    columns = (block * KC_DEV + parent_map).astype(jnp.int32)
    centroids = coarse_centroids[:, columns] + fine_offsets
    owner = fragment_owner[:, 0]
    span = N_XY * KF_DEV
    column_owner = jnp.arange(span, dtype=jnp.int32) // KF_DEV
    pseudo = float(PSEUDO)

    for step in range(ITERS):
        def visit(carry, device):
            numer, denom = carry
            row_start = ((device // N_XY) * span).astype(jnp.int32)
            frag_start = (device * FL).astype(jnp.int32)
            frags = lax.dynamic_slice_in_dim(fragment_means, frag_start, FL, 1)
            weight = lax.dynamic_slice_in_dim(voxel_count, frag_start, FL, 0)
            own = lax.dynamic_slice_in_dim(owner, frag_start, FL, 0)
            cents = lax.dynamic_slice_in_dim(centroids, row_start, span, 1)
            part_num, part_den = soft_stats(frags, weight, cents, own[:, None] == column_owner[None, :])
            numer = lax.dynamic_update_slice_in_dim(numer, lax.dynamic_slice_in_dim(numer, row_start, span, 1) + part_num, row_start, 1)
            denom = lax.dynamic_update_slice_in_dim(denom, lax.dynamic_slice_in_dim(denom, row_start, span, 0) + part_den, row_start, 0)
            return (numer, denom), None

        start_carry = (jnp.zeros((CH, KF), jnp.float32), jnp.zeros((KF,), jnp.float32))
        carried = lax.scan(visit, start_carry, jnp.arange(N_GZ * N_XY, dtype=jnp.int32))[0]
        centroids = (carried[0] + pseudo * centroids) / (carried[1][None, :] + pseudo)
    return fragment_means, centroids
```

```python
import functools

import jax
import jax.numpy as jnp
from jax import lax
from jax.experimental import pallas as pl
from jax.experimental.pallas import tpu as pltpu
from jax.sharding import PartitionSpec as P

TAPS = 5
HALF = TAPS // 2
ITERS = 3
HIGH = lax.Precision.HIGHEST
sharpness = 2.0
LO = 128
ROWS = 16
F32 = jnp.float32
BF16 = jnp.bfloat16


MESH = pl.DeviceIdType.MESH
LANE = 128
GROUP = 24


def exchange_kernel(rows, img, out, blocks, edges, halo, turned, send, recv, side_send, side_recv):
    here = lax.axis_index("gz")
    lane = lax.axis_index("xy")
    stacks = lax.axis_size("gz")
    lanes = lax.axis_size("xy")
    depth, height, cols = img.shape
    padded = rows + TAPS - 1
    size = depth * padded
    wide = depth * HALF

    def clear(i, carry):
        at = pl.ds(pl.multiple_of(i * 8, 8), 8)
        out[at, :LANE] = jnp.zeros((8, LANE), F32)
        out[at, LANE + cols :] = jnp.zeros((8, LANE), F32)
        return carry

    lax.fori_loop(0, stacks * size // 8, clear, 0)

    for side in range(2):
        if stacks * wide < LANE:
            halo[side, stacks * wide :, :] = jnp.zeros((LANE - stacks * wide, height), F32)

    @pl.when(lane == 0)
    def _():
        halo[0] = jnp.zeros(halo.shape[1:], F32)

    @pl.when(lane == lanes - 1)
    def _():
        halo[1] = jnp.zeros(halo.shape[1:], F32)

    barrier = pltpu.get_barrier_semaphore()

    def greet(d, carry):
        j = lax.rem(here + d, stacks)

        @pl.when(d > 0)
        def _():
            pl.semaphore_signal(barrier, inc=1, device_id=(j, lane), device_id_type=MESH)

        @pl.when(lane > 0)
        def _():
            pl.semaphore_signal(barrier, inc=1, device_id=(j, lane - 1), device_id_type=MESH)

        @pl.when(lane < lanes - 1)
        def _():
            pl.semaphore_signal(barrier, inc=1, device_id=(j, lane + 1), device_id_type=MESH)

        return carry

    lax.fori_loop(0, stacks, greet, 0)
    for j in range(stacks):
        for z in range(depth):
            start = j * rows - HALF
            low, high = max(start, 0), min(start + padded, height)
            at = z * padded
            if low > start:
                blocks[j, at : at + low - start, :] = jnp.zeros((low - start, cols), F32)
            if high < start + padded:
                blocks[j, at + high - start : at + padded, :] = jnp.zeros(
                    (start + padded - high, cols), F32
                )
            blocks[j, at + low - start : at + high - start, :] = img[z, low:high, :]
    for z in range(depth):
        first = jnp.transpose(img[z, :, :LANE])
        last = jnp.transpose(img[z, :, cols - LANE :])
        edges[0, z * HALF : (z + 1) * HALF, :] = last[LANE - HALF :, :]
        edges[1, z * HALF : (z + 1) * HALF, :] = first[:HALF, :]
    sides = lax.div(lane + lanes - 1, lanes) + lax.div(2 * lanes - 2 - lane, lanes)
    pl.semaphore_wait(barrier, stacks - 1 + stacks * sides)

    def main_copy(j, source):
        return pltpu.make_async_remote_copy(
            src_ref=blocks.at[j],
            dst_ref=out.at[pl.ds(pl.multiple_of(source * size, 8), size), LANE : LANE + cols],
            send_sem=send.at[j],
            recv_sem=recv.at[source],
            device_id=(j, lane),
            device_id_type=MESH,
        )

    def side_copy(side, j, source, target):
        return pltpu.make_async_remote_copy(
            src_ref=edges.at[side],
            dst_ref=halo.at[side, pl.ds(pl.multiple_of(source * wide, 8), wide), :],
            send_sem=side_send.at[side, j],
            recv_sem=side_recv.at[side, source],
            device_id=(j, target),
            device_id_type=MESH,
        )

    def start(d, carry):
        j = lax.rem(here + d, stacks)

        @pl.when(d > 0)
        def _():
            main_copy(j, here).start()

        @pl.when(lane < lanes - 1)
        def _():
            side_copy(0, j, here, lane + 1).start()

        @pl.when(lane > 0)
        def _():
            side_copy(1, j, here, lane - 1).start()

        return carry

    lax.fori_loop(0, stacks, start, 0)
    out[pl.ds(pl.multiple_of(here * size, 8), size), LANE : LANE + cols] = blocks[here]

    def finish(d, carry):
        j = lax.rem(here + d, stacks)

        @pl.when(d > 0)
        def _():
            main_copy(j, here).wait_send()
            main_copy(j, j).wait_recv()

        @pl.when(lane < lanes - 1)
        def _():
            side_copy(0, j, here, lane + 1).wait_send()
            side_copy(1, j, j, lane + 1).wait_recv()

        @pl.when(lane > 0)
        def _():
            side_copy(1, j, here, lane - 1).wait_send()
            side_copy(0, j, j, lane - 1).wait_recv()

        return carry

    lax.fori_loop(0, stacks, finish, 0)
    out[stacks * size :, :] = jnp.zeros((out.shape[0] - stacks * size, out.shape[1]), F32)
    for side in range(2):
        turned[:8, :] = jnp.zeros((8, LANE), F32)
        turned[8 + height :, :] = jnp.zeros((8, LANE), F32)
        turned[8 : 8 + height, :] = jnp.transpose(halo[side])
        strip = turned[pl.ds(here * rows + 8 - HALF, padded), :]
        for z in range(stacks * depth):
            place = LANE - HALF if side == 0 else LANE + cols
            out[z * padded : (z + 1) * padded, place : place + HALF] = strip[
                :, z * HALF : (z + 1) * HALF
            ]


def gather_kernel(pay, out, send, recv):
    here = lax.axis_index("gz")
    lane = lax.axis_index("xy")
    lanes = lax.axis_size("xy")
    barrier = pltpu.get_barrier_semaphore()
    for d in range(1, lanes):
        pl.semaphore_signal(
            barrier, inc=1, device_id=(here, lax.rem(lane + d, lanes)), device_id_type=MESH
        )
    pl.semaphore_wait(barrier, lanes - 1)

    def copy(target, source):
        return pltpu.make_async_remote_copy(
            src_ref=pay,
            dst_ref=out.at[source],
            send_sem=send.at[target],
            recv_sem=recv.at[source],
            device_id=(here, target),
            device_id_type=MESH,
        )

    for d in range(1, lanes):
        copy(lax.rem(lane + d, lanes), lane).start()
    out[lane] = pay[...]
    for d in range(1, lanes):
        other = lax.rem(lane + d, lanes)
        copy(other, lane).wait_send()
        copy(other, other).wait_recv()


def feature_kernel(
    img, ids, wide, tall, deep, owner, pay_ref, means_ref,
    planar, highs_f, lows_f, acc, square, filt,
):
    depth, rows, cols = ids.shape
    padded_rows = rows + TAPS - 1
    fragments = means_ref.shape[1]
    highs = fragments // LO
    chans = means_ref.shape[0]
    lanes = pay_ref.shape[0] - chans
    for e in range(HALF):
        planar[e] = jnp.zeros(planar.shape[1:], F32)
        planar[depth + HALF + e] = jnp.zeros(planar.shape[1:], F32)
    acc[...] = jnp.zeros(acc.shape, F32)

    def divide(z, carry):
        for x in range(0, cols, LANE):
            part = ids[z, :, x : x + LANE]
            highs_f[x // LANE, z] = (part >> (LO.bit_length() - 1)).astype(F32)
            lows_f[x // LANE, z] = (part & (LO - 1)).astype(F32)
        return carry

    lax.fori_loop(0, depth, divide, 0)
    square[...] = jnp.zeros(square.shape, F32)
    for kind, part in enumerate((wide, tall, deep)):
        square[kind * 8 : kind * 8 + TAPS, :chans] = part[...]
    turned = jnp.transpose(square[...])
    tap = [
        jnp.broadcast_to(turned[:chans, k * 8 + i : k * 8 + i + 1], (chans, LANE))
        for k in range(3)
        for i in range(TAPS)
    ]
    line = lax.broadcasted_iota(jnp.int32, (chans, LANE), 1)
    shift_of = line // GROUP
    row_of = line % GROUP
    across = jnp.zeros((chans, LANE), F32)
    for b in range(TAPS):
        across = jnp.where(shift_of == b, tap[b], across)
    for y in range(rows):
        down = jnp.zeros((chans, LANE), F32)
        for a in range(TAPS):
            down = jnp.where(row_of == y + a, tap[TAPS + a], down)
        both = across * down
        high = both.astype(BF16)
        low = (both - high.astype(F32)).astype(BF16)
        filt[y * chans : (y + 1) * chans, :LANE] = high
        filt[y * chans : (y + 1) * chans, LANE : 2 * LANE] = low
        filt[y * chans : (y + 1) * chans, 2 * LANE : 3 * LANE] = high
        filt[y * chans : (y + 1) * chans, 3 * LANE :] = low

    thick = 4

    def plane(slab, carry):
        size = thick * padded_rows
        view = img.at[pl.ds(pl.multiple_of(slab * size, 8), size + 8), :]
        for k in range(thick):
            block = view[k * padded_rows : k * padded_rows + GROUP, :]
            top, low = [], []
            for b in range(TAPS):
                start = LANE - HALF + b
                part = block[:, start : start + cols]
                high = part.astype(BF16).astype(F32)
                top.append(high)
                low.append(part - high)
            rest = jnp.zeros((LANE - TAPS * GROUP, cols), F32)
            top = jnp.concatenate(top + [rest], axis=0).astype(BF16)
            low = jnp.concatenate(low + [rest], axis=0).astype(BF16)
            total = jnp.dot(
                filt[...], jnp.concatenate([top, top, low, low], axis=0), preferred_element_type=F32
            )
            planar[slab * thick + k + HALF] = total.astype(BF16).astype(F32)
        return carry

    lax.fori_loop(0, depth // thick, plane, 0)
    low_line = lax.broadcasted_iota(jnp.int32, (LO, LANE), 0).astype(F32).astype(BF16)
    one = jnp.ones((16, LANE), BF16)
    zero = jnp.zeros((16, LANE), BF16)

    def count(z, carry):
        left, right = [], []
        for y in range(rows):
            for x in range(0, cols, LANE):
                at = slice(y * chans, (y + 1) * chans)
                total = tap[2 * TAPS] * planar[z, at, x : x + LANE]
                for e in range(1, TAPS):
                    total = total + tap[2 * TAPS + e] * planar[z + e, at, x : x + LANE]
                feat = jnp.tanh(total).astype(BF16)
                high = highs_f[x // LANE, z, pl.ds(y, 1), :]
                high = jnp.broadcast_to(high, (16, LANE)).astype(BF16)
                low = lows_f[x // LANE, z, pl.ds(y, 1), :]
                low = jnp.broadcast_to(low, (16, LANE)).astype(BF16)
                left.append(jnp.concatenate(
                    [jnp.where(high == jnp.full((16, LANE), h, BF16), feat, zero) for h in range(highs)]
                    + [jnp.where(high == low_line[:16], one, zero)],
                    axis=0,
                ))
                right.append(jnp.concatenate(
                    [jnp.where(low == low_line[k * 16 : (k + 1) * 16], one, zero) for k in range(LO // 16)],
                    axis=0,
                ))
        acc[...] += lax.dot_general(
            jnp.concatenate(left, axis=1), jnp.concatenate(right, axis=1),
            (((1,), (1,)), ((), ())), preferred_element_type=F32,
        )
        return carry

    lax.fori_loop(0, depth, count, 0)
    for h in range(highs):
        count = acc[highs * chans + h : highs * chans + h + 1, :]
        mean = acc[h * chans : (h + 1) * chans, :] / count
        means_ref[:, h * LO : (h + 1) * LO] = mean
        pay_ref[:chans, h * LO : (h + 1) * LO] = mean
        own = jnp.broadcast_to(owner[:, h * LO : (h + 1) * LO], (lanes, LO))
        line = lax.broadcasted_iota(jnp.int32, (lanes, LO), 0)
        pay_ref[chans:, h * LO : (h + 1) * LO] = jnp.where(
            own == line, jnp.broadcast_to(count, (lanes, LO)), 0.0
        )


def split3(x):
    high = x.astype(BF16)
    rest = x - high.astype(F32)
    mid = rest.astype(BF16)
    low = (rest - mid.astype(F32)).astype(BF16)
    return high, mid, low


def refine_kernel(pseudo, pay, coarse, parent, offsets, out_ref, factors, norms):
    sources, _, fragments = pay.shape
    chans = out_ref.shape[0]
    own = chans + lax.axis_index("xy")
    coarse_count = coarse.shape[1]
    fine = out_ref.shape[1]
    select = (
        jnp.broadcast_to(parent[...], (coarse_count, fine))
        == lax.broadcasted_iota(jnp.int32, (coarse_count, fine), 0)
    ).astype(F32)
    cents = jnp.dot(coarse[...], select, precision=HIGH, preferred_element_type=F32) + offsets[...]

    def prepare(s, carry):
        frags = pay[s, :chans, :]
        fh, fm, fl = split3(-2.0 * frags)
        ones = jnp.ones((3 * chans, fragments), BF16)
        factors[s] = jnp.concatenate([fh, fm, fh, fl, fm, fh, ones], axis=0)
        norms[s] = jnp.sum(frags * frags, axis=0, keepdims=True)
        return carry

    lax.fori_loop(0, sources, prepare, 0, unroll=4)
    for step in range(ITERS):
        ch, cm, cl = split3(cents)
        sh, sm, sl = split3(cents * cents)
        keys = jnp.concatenate([ch, ch, cm, ch, cm, cl, sh, sm, sl], axis=0)

        def visit(s, total):
            distance = norms[s] + lax.dot_general(
                keys, factors[s], (((0,), (0,)), ((), ())), preferred_element_type=F32
            )
            scores = -sharpness * distance
            top = jnp.max(scores, axis=0, keepdims=True)
            expo = jnp.exp(scores - top)
            scale = pay[s, pl.ds(own, 1), :] / jnp.sum(expo, axis=0, keepdims=True)
            scale = jnp.broadcast_to(scale, (chans, fragments))
            gh, gm, gl = split3(jnp.concatenate([pay[s, :chans, :] * scale, scale], axis=0))
            eh, em, el = split3(expo)
            dims = (((1,), (1,)), ((), ()))
            first = lax.dot_general(
                jnp.concatenate([gh, gm, gl], axis=0), eh, dims, preferred_element_type=F32
            )
            second = lax.dot_general(
                jnp.concatenate([gh, gm], axis=0), em, dims, preferred_element_type=F32
            )
            size = 2 * chans
            return (
                total
                + (first[2 * size :] + second[size:])
                + (first[size : 2 * size] + second[:size])
                + first[:size]
            )

        total = lax.fori_loop(
            0, sources, visit, jnp.zeros((2 * chans, fine), F32), unroll=4
        )
        cents = (total[:chans] + pseudo * cents) / (total[chans:] + pseudo)
    out_ref[...] = cents


def shards(
    slab_image,
    width_taps,
    height_taps,
    depth_taps,
    fragment_ids,
    fragment_owner,
    coarse_centroids,
    parent_map,
    fine_offsets,
):
    chans = width_taps.shape[0]
    depth, rows, cols = fragment_ids.shape
    fragments = fragment_owner.shape[0]
    lanes = lax.axis_size("xy")
    stacks = lax.axis_size("gz")
    padded_rows = rows + TAPS - 1
    slab_depth, height, _ = slab_image.shape
    pencil = pl.pallas_call(
        functools.partial(exchange_kernel, rows),
        out_shape=jax.ShapeDtypeStruct((depth * padded_rows + 8, cols + 2 * LANE), F32),
        in_specs=[pl.BlockSpec(memory_space=pltpu.VMEM)],
        out_specs=pl.BlockSpec(memory_space=pltpu.VMEM),
        scratch_shapes=[
            pltpu.VMEM((stacks, slab_depth * padded_rows, cols), F32),
            pltpu.VMEM((2, slab_depth * HALF, height), F32),
            pltpu.VMEM((2, LANE, height), F32),
            pltpu.VMEM((height + 16, LANE), F32),
            pltpu.SemaphoreType.DMA((stacks,)),
            pltpu.SemaphoreType.DMA((stacks,)),
            pltpu.SemaphoreType.DMA((2, stacks)),
            pltpu.SemaphoreType.DMA((2, stacks)),
        ],
        compiler_params=pltpu.CompilerParams(
            collective_id=0, has_side_effects=True, vmem_limit_bytes=32 << 20
        ),
        name="exchange",
    )(slab_image)
    highs = fragments // LO
    assert highs <= 16
    grant = (16 << 20) + 144 * depth * rows * cols
    pay, means = pl.pallas_call(
        feature_kernel,
        out_shape=(
            jax.ShapeDtypeStruct((chans + lanes, fragments), F32),
            jax.ShapeDtypeStruct((chans, fragments), F32),
        ),
        in_specs=[pl.BlockSpec(memory_space=pltpu.VMEM)] * 6,
        out_specs=(pl.BlockSpec(memory_space=pltpu.VMEM),) * 2,
        scratch_shapes=[
            pltpu.VMEM((depth + 2 * HALF, rows * chans, cols), F32),
            pltpu.VMEM((cols // LANE, depth, rows, LANE), F32),
            pltpu.VMEM((cols // LANE, depth, rows, LANE), F32),
            pltpu.VMEM((highs * chans + 16, LO), F32),
            pltpu.VMEM((LANE, LANE), F32),
            pltpu.VMEM((rows * chans, 4 * LANE), BF16),
        ],
        compiler_params=pltpu.CompilerParams(vmem_limit_bytes=grant),
        name="features",
    )(pencil, fragment_ids, width_taps.T, height_taps.T, depth_taps.T, fragment_owner.reshape(1, fragments))
    gathered = pl.pallas_call(
        gather_kernel,
        out_shape=jax.ShapeDtypeStruct((lanes,) + pay.shape, F32),
        in_specs=[pl.BlockSpec(memory_space=pltpu.VMEM)],
        out_specs=pl.BlockSpec(memory_space=pltpu.VMEM),
        scratch_shapes=[pltpu.SemaphoreType.DMA((lanes,)), pltpu.SemaphoreType.DMA((lanes,))],
        compiler_params=pltpu.CompilerParams(
            collective_id=1, has_side_effects=True, vmem_limit_bytes=16 << 20
        ),
        name="gather",
    )(pay)
    fine = fine_offsets.shape[1]
    pseudo = float(fragment_ids.size // fine)
    centroids = pl.pallas_call(
        functools.partial(refine_kernel, pseudo),
        out_shape=jax.ShapeDtypeStruct((chans, fine), F32),
        in_specs=[pl.BlockSpec(memory_space=pltpu.VMEM)] * 4,
        out_specs=pl.BlockSpec(memory_space=pltpu.VMEM),
        scratch_shapes=[
            pltpu.VMEM((lanes, 9 * chans, fragments), BF16),
            pltpu.VMEM((lanes, 1, fragments), F32),
        ],
        compiler_params=pltpu.CompilerParams(vmem_limit_bytes=48 << 20),
        name="refine",
    )(gathered, coarse_centroids, parent_map.reshape(1, fine), fine_offsets)
    return (means, centroids)


def solution(mesh):
    placed = (
        P("gz", None, "xy"),
        P(),
        P(),
        P(),
        P(None, "gz", "xy"),
        P(("gz", "xy"), None),
        P(None, ("gz", "xy")),
        P(("gz", "xy")),
        P(None, ("gz", "xy")),
    )
    return jax.shard_map(
        shards,
        mesh=mesh,
        in_specs=placed,
        out_specs=(P(None, ("gz", "xy")), P(None, ("gz", "xy"))),
        check_vma=False,
    )
```

```python
import functools

import jax
import jax.numpy as jnp
from jax import lax
from jax.experimental import pallas as pl
from jax.experimental.pallas import tpu as pltpu
from jax.sharding import PartitionSpec as P

TAPS = 5
HALF = TAPS // 2
ITERS = 3
HIGH = lax.Precision.HIGHEST
sharpness = 2.0
LO = 128
F32 = jnp.float32
BF16 = jnp.bfloat16


MESH = pl.DeviceIdType.MESH
LANE = 128
PART = 16
SPREAD = 240.0


def encode(x):
    return jnp.exp2((x - 0.5) * SPREAD)


def decode(x):
    return jnp.log2(x) * (1.0 / SPREAD) + 0.5


def pencil_kernel(
    img, ids, wide, tall, deep, owner, pay_ref, means_ref,
    image, blocks, came, pack, edges, halo, turned, square, filt,
    planar, whole_ids, highs_f, lows_f, acc,
    load, send, recv, side_send, side_recv,
):
    here = lax.axis_index("gz")
    lane = lax.axis_index("xy")
    stacks = lax.axis_size("gz")
    lanes = lax.axis_size("xy")
    thick, height, cols = img.shape
    depth, rows, _ = ids.shape
    padded = rows + TAPS - 1
    size = thick * padded
    wide_rows = thick * HALF
    chans, fragments = means_ref.shape
    highs = fragments // LO

    img_load = pltpu.make_async_copy(img, image.at[:, pl.ds(8, height), :], load.at[0])
    ids_load = pltpu.make_async_copy(ids, whole_ids, load.at[1])
    img_load.start()
    ids_load.start()

    barrier = pltpu.get_barrier_semaphore()

    def greet(d, carry):
        j = lax.rem(here + d, stacks)

        @pl.when(d > 0)
        def _():
            pl.semaphore_signal(barrier, inc=1, device_id=(j, lane), device_id_type=MESH)

        @pl.when(lane > 0)
        def _():
            pl.semaphore_signal(barrier, inc=1, device_id=(j, lane - 1), device_id_type=MESH)

        @pl.when(lane < lanes - 1)
        def _():
            pl.semaphore_signal(barrier, inc=1, device_id=(j, lane + 1), device_id_type=MESH)

        return carry

    lax.fori_loop(0, stacks, greet, 0)

    @pl.when(lane == 0)
    def _():
        halo[0] = jnp.zeros(halo.shape[1:], F32)

    @pl.when(lane == lanes - 1)
    def _():
        halo[1] = jnp.zeros(halo.shape[1:], F32)

    blank = encode(jnp.zeros((thick, 8, cols), F32))
    image[:, :8, :] = blank
    image[:, 8 + height :, :] = blank
    pack[size:, :] = blank[0]
    turned[:8, :] = jnp.zeros((8, LANE), F32)
    turned[8 + height :, :] = jnp.zeros((8, LANE), F32)
    square[...] = jnp.zeros(square.shape, F32)
    img_load.wait()
    spot = lax.broadcasted_iota(jnp.int32, (LANE, LANE), 1)
    for y in range(0, height, LANE):
        mixed = jnp.zeros((LANE, LANE), F32)
        for z in range(thick):
            first = image[z, 8 + y : 8 + y + LANE, :LANE]
            last = image[z, 8 + y : 8 + y + LANE, cols - LANE :]
            at = z * HALF
            mixed = jnp.where((spot >= at) & (spot < at + HALF), pltpu.roll(last, (at + HALF) % LANE, 1), mixed)
            at = wide_rows + z * HALF
            mixed = jnp.where((spot >= at) & (spot < at + HALF), pltpu.roll(first, at, 1), mixed)
        both = jnp.transpose(mixed)
        edges[0, :, y : y + LANE] = both[:wide_rows]
        edges[1, :, y : y + LANE] = both[wide_rows : 2 * wide_rows]

    def code(i, carry):
        at = pl.ds(pl.multiple_of(8 + i * 32, 8), 32)
        for z in range(thick):
            image[z, at, :] = encode(image[z, at, :])
        return carry

    lax.fori_loop(0, height // 32, code, 0)

    def main_copy(j, source):
        return pltpu.make_async_remote_copy(
            src_ref=blocks.at[j],
            dst_ref=came.at[source],
            send_sem=send.at[j],
            recv_sem=recv.at[source],
            device_id=(j, lane),
            device_id_type=MESH,
        )

    def side_copy(side, j, source, target):
        return pltpu.make_async_remote_copy(
            src_ref=edges.at[side],
            dst_ref=halo.at[side, source],
            send_sem=side_send.at[side, j],
            recv_sem=side_recv.at[side, source],
            device_id=(j, target),
            device_id_type=MESH,
        )

    sides = lax.div(lane + lanes - 1, lanes) + lax.div(2 * lanes - 2 - lane, lanes)
    pl.semaphore_wait(barrier, stacks - 1 + stacks * sides)

    def build(j, ref):
        for z in range(thick):
            view = image.at[z, pl.ds(pl.multiple_of(j * rows, 8), rows + 16), :]
            pack[z * padded : (z + 1) * padded, :] = view[8 - HALF : 8 - HALF + padded, :]
        ref[...] = pack[:size, :].astype(BF16)

    def start(d, carry):
        hop = (d + 1) // 2
        j = lax.rem(here + stacks + jnp.where(d % 2 == 1, hop, -hop), stacks)

        @pl.when(lane < lanes - 1)
        def _():
            side_copy(0, j, here, lane + 1).start()

        @pl.when(lane > 0)
        def _():
            side_copy(1, j, here, lane - 1).start()

        build(j, blocks.at[j])

        @pl.when(d > 0)
        def _():
            main_copy(j, here).start()

        return carry

    lax.fori_loop(0, stacks, start, 0)
    came[here] = blocks[here]

    for e in range(HALF):
        planar[e] = jnp.zeros(planar.shape[1:], F32)
        planar[depth + HALF + e] = jnp.zeros(planar.shape[1:], F32)
    acc[...] = jnp.zeros(acc.shape, F32)
    ids_load.wait()

    def divide(z, carry):
        for x in range(0, cols, LANE):
            part = whole_ids[z, :, x : x + LANE]
            highs_f[x // LANE, z] = (part >> (LO.bit_length() - 1)).astype(F32)
            lows_f[x // LANE, z] = (part & (LO - 1)).astype(F32)
        return carry

    lax.fori_loop(0, depth, divide, 0)
    for kind, part in enumerate((wide, tall, deep)):
        square[kind * 8 : kind * 8 + TAPS, :chans] = part[...]
    flipped = jnp.transpose(square[...])
    tap = [
        jnp.broadcast_to(flipped[:chans, k * 8 + i : k * 8 + i + 1], (chans, LANE))
        for k in range(3)
        for i in range(TAPS)
    ]
    group = TAPS * PART
    half_rows = PART // 2
    for t in range(2):
        line = lax.broadcasted_iota(jnp.int32, (chans, LANE), 1) + t * LANE
        shift_of = line % group // PART
        row_of = line % PART
        kind_of = line // group
        across = jnp.zeros((chans, LANE), F32)
        for b in range(TAPS):
            across = jnp.where((shift_of == b) & (kind_of < 3), tap[b], across)
        for y in range(half_rows):
            down = jnp.zeros((chans, LANE), F32)
            for a in range(TAPS):
                down = jnp.where(row_of == y + a, tap[TAPS + a], down)
            both = across * down
            high = both.astype(BF16)
            low = (both - high.astype(F32)).astype(BF16)
            filt[y * chans : (y + 1) * chans, t * LANE : (t + 1) * LANE] = jnp.where(
                kind_of == 1, low.astype(F32), high.astype(F32)
            ).astype(BF16)

    def plane(slab):
        turned[8 : 8 + height, :] = jnp.concatenate(
            [
                jnp.transpose(
                    jnp.concatenate(
                        [halo[0, slab, :, y : y + LANE], halo[1, slab, :, y : y + LANE],
                         jnp.zeros((LANE - 2 * wide_rows, LANE), F32)],
                        axis=0,
                    )
                )
                for y in range(0, height, LANE)
            ],
            axis=0,
        )
        strip = turned[pl.ds(here * rows + 8 - HALF, 24), :]
        pack[:size, :] = decode(came[slab].astype(F32))
        for z in range(thick):
            block = pack[z * padded : z * padded + 24, :]
            ends = [
                pltpu.roll(strip, (LANE - HALF - z * HALF) % LANE, 1),
                pltpu.roll(strip, (LANE - wide_rows - z * HALF) % LANE, 1),
            ]
            block = jnp.concatenate([ends[0], block, ends[1]], axis=1)
            top, low = [], []
            for b in range(TAPS):
                part = block[:, LANE - HALF + b : LANE - HALF + b + cols]
                high = part.astype(BF16).astype(F32)
                top.append(high)
                low.append(part - high)
            rest = jnp.zeros((2 * LANE - 3 * group, cols), BF16)
            for y in range(0, rows, half_rows):
                upper = jnp.concatenate([t[y : y + PART] for t in top], axis=0).astype(BF16)
                lower = jnp.concatenate([t[y : y + PART] for t in low], axis=0).astype(BF16)
                total = jnp.dot(
                    filt[...], jnp.concatenate([upper, upper, lower, rest], axis=0),
                    preferred_element_type=F32,
                )
                planar[slab * thick + z + HALF, y * chans : (y + half_rows) * chans, :] = (
                    total.astype(BF16).astype(F32)
                )

    low_line = lax.broadcasted_iota(jnp.int32, (LO, LANE), 0).astype(F32).astype(BF16)
    high_line = (lax.broadcasted_iota(jnp.int32, (highs * chans, LANE), 0) // chans).astype(F32).astype(BF16)
    one = jnp.ones((LO, LANE), BF16)
    zero = jnp.zeros((LO, LANE), BF16)
    none = jnp.zeros((highs * chans, LANE), BF16)

    def count(z):
        left, right = [], []
        for y in range(rows):
            for x in range(0, cols, LANE):
                at = slice(y * chans, (y + 1) * chans)
                total = tap[2 * TAPS] * planar[z, at, x : x + LANE]
                for e in range(1, TAPS):
                    total = total + tap[2 * TAPS + e] * planar[z + e, at, x : x + LANE]
                feat = jnp.tanh(total).astype(BF16)
                high = highs_f[x // LANE, z, pl.ds(y, 1), :]
                high = jnp.broadcast_to(high, (16, LANE)).astype(BF16)
                low = lows_f[x // LANE, z, pl.ds(y, 1), :]
                low = jnp.broadcast_to(low, (16, LANE)).astype(BF16)
                left.append(jnp.concatenate(
                    [jnp.where(jnp.concatenate([high] * highs, axis=0) == high_line,
                               jnp.concatenate([feat] * highs, axis=0), none),
                     jnp.where(high == low_line[:16], one[:16], zero[:16])],
                    axis=0,
                ))
                right.append(jnp.where(jnp.concatenate([low] * (LO // 16), axis=0) == low_line, one, zero))
        return left, right

    def tally(slab):
        left, right = [], []
        for z in range(thick):
            parts = count(slab * thick + z)
            left += parts[0]
            right += parts[1]
        acc[...] += lax.dot_general(
            jnp.concatenate(left, axis=1), jnp.concatenate(right, axis=1),
            (((1,), (1,)), ((), ())), preferred_element_type=F32,
        )

    def arrive(slab):
        @pl.when(slab != here)
        def _():
            main_copy(slab, slab).wait_recv()

        @pl.when(lane < lanes - 1)
        def _():
            side_copy(1, slab, slab, lane + 1).wait_recv()

        @pl.when(lane > 0)
        def _():
            side_copy(0, slab, slab, lane - 1).wait_recv()

    way = jnp.where(2 * here < stacks, 1, -1)

    def place(i):
        return lax.rem(here + way * i + 2 * stacks, stacks)

    def prepare(i, carry):
        slab = place(i)
        arrive(slab)
        plane(slab)
        return carry

    lax.fori_loop(0, 2, prepare, 0)
    behind = here - way
    last = place(stacks - 1)
    early = jnp.logical_and(behind >= 0, behind < stacks)

    @pl.when(early)
    def _():
        prepare(stacks - 1, 0)

    def work(i, carry):
        tally(place(i))

        @pl.when(i + 2 < stacks - 1)
        def _():
            prepare(i + 2, 0)

        @pl.when(jnp.logical_and(i + 2 == stacks - 1, jnp.logical_not(early)))
        def _():
            prepare(i + 2, 0)

        return carry

    lax.fori_loop(0, stacks, work, 0)

    def finish(d, carry):
        j = lax.rem(here + d, stacks)

        @pl.when(d > 0)
        def _():
            main_copy(j, here).wait_send()

        @pl.when(lane < lanes - 1)
        def _():
            side_copy(0, j, here, lane + 1).wait_send()

        @pl.when(lane > 0)
        def _():
            side_copy(1, j, here, lane - 1).wait_send()

        return carry

    lax.fori_loop(0, stacks, finish, 0)
    for h in range(highs):
        count_row = acc[highs * chans + h : highs * chans + h + 1, :]
        mean = acc[h * chans : (h + 1) * chans, :] / count_row
        means_ref[:, h * LO : (h + 1) * LO] = mean
        pay_ref[:chans, h * LO : (h + 1) * LO] = mean
        own = jnp.broadcast_to(owner[:, h * LO : (h + 1) * LO], (lanes, LO))
        line = lax.broadcasted_iota(jnp.int32, (lanes, LO), 0)
        pay_ref[chans:, h * LO : (h + 1) * LO] = jnp.where(
            own == line, jnp.broadcast_to(count_row, (lanes, LO)), 0.0
        )


def gather_kernel(pay, out, send, recv):
    here = lax.axis_index("gz")
    lane = lax.axis_index("xy")
    lanes = lax.axis_size("xy")
    barrier = pltpu.get_barrier_semaphore()
    for d in range(1, lanes):
        pl.semaphore_signal(
            barrier, inc=1, device_id=(here, lax.rem(lane + d, lanes)), device_id_type=MESH
        )
    pl.semaphore_wait(barrier, lanes - 1)

    def copy(target, source):
        return pltpu.make_async_remote_copy(
            src_ref=pay,
            dst_ref=out.at[source],
            send_sem=send.at[target],
            recv_sem=recv.at[source],
            device_id=(here, target),
            device_id_type=MESH,
        )

    for d in range(1, lanes):
        copy(lax.rem(lane + d, lanes), lane).start()
    out[lane] = pay[...]
    for d in range(1, lanes):
        other = lax.rem(lane + d, lanes)
        copy(other, lane).wait_send()
        copy(other, other).wait_recv()


def split3(x):
    high = x.astype(BF16)
    rest = x - high.astype(F32)
    mid = rest.astype(BF16)
    low = (rest - mid.astype(F32)).astype(BF16)
    return high, mid, low


def refine_kernel(pseudo, pay, coarse, parent, offsets, out_ref, factors, norms):
    sources, _, fragments = pay.shape
    chans = out_ref.shape[0]
    own = chans + lax.axis_index("xy")
    coarse_count = coarse.shape[1]
    fine = out_ref.shape[1]
    select = (
        jnp.broadcast_to(parent[...], (coarse_count, fine))
        == lax.broadcasted_iota(jnp.int32, (coarse_count, fine), 0)
    ).astype(F32)
    cents = jnp.dot(coarse[...], select, precision=HIGH, preferred_element_type=F32) + offsets[...]

    def prepare(s, carry):
        frags = pay[s, :chans, :]
        fh, fm, fl = split3(-2.0 * frags)
        ones = jnp.ones((3 * chans, fragments), BF16)
        factors[s] = jnp.concatenate([fh, fm, fh, fl, fm, fh, ones], axis=0)
        norms[s] = jnp.sum(frags * frags, axis=0, keepdims=True)
        return carry

    lax.fori_loop(0, sources, prepare, 0, unroll=4)
    for step in range(ITERS):
        ch, cm, cl = split3(cents)
        sh, sm, sl = split3(cents * cents)
        keys = jnp.concatenate([ch, ch, cm, ch, cm, cl, sh, sm, sl], axis=0)

        def visit(s, total):
            distance = norms[s] + lax.dot_general(
                keys, factors[s], (((0,), (0,)), ((), ())), preferred_element_type=F32
            )
            scores = -sharpness * distance
            top = jnp.max(scores, axis=0, keepdims=True)
            expo = jnp.exp(scores - top)
            scale = pay[s, pl.ds(own, 1), :] / jnp.sum(expo, axis=0, keepdims=True)
            scale = jnp.broadcast_to(scale, (chans, fragments))
            gh, gm, gl = split3(jnp.concatenate([pay[s, :chans, :] * scale, scale], axis=0))
            eh, em, el = split3(expo)
            dims = (((1,), (1,)), ((), ()))
            first = lax.dot_general(
                jnp.concatenate([gh, gm, gl], axis=0), eh, dims, preferred_element_type=F32
            )
            second = lax.dot_general(
                jnp.concatenate([gh, gm], axis=0), em, dims, preferred_element_type=F32
            )
            size = 2 * chans
            return (
                total
                + (first[2 * size :] + second[size:])
                + (first[size : 2 * size] + second[:size])
                + first[:size]
            )

        total = lax.fori_loop(
            0, sources, visit, jnp.zeros((2 * chans, fine), F32), unroll=4
        )
        cents = (total[:chans] + pseudo * cents) / (total[chans:] + pseudo)
    out_ref[...] = cents


def shards(
    slab_image,
    width_taps,
    height_taps,
    depth_taps,
    fragment_ids,
    fragment_owner,
    coarse_centroids,
    parent_map,
    fine_offsets,
):
    chans = width_taps.shape[0]
    depth, rows, cols = fragment_ids.shape
    fragments = fragment_owner.shape[0]
    lanes = lax.axis_size("xy")
    stacks = lax.axis_size("gz")
    padded_rows = rows + TAPS - 1
    slab_depth, height, _ = slab_image.shape
    highs = fragments // LO
    assert highs <= 16
    pay, means = pl.pallas_call(
        pencil_kernel,
        out_shape=(
            jax.ShapeDtypeStruct((chans + lanes, fragments), F32),
            jax.ShapeDtypeStruct((chans, fragments), F32),
        ),
        in_specs=[pl.BlockSpec(memory_space=pl.ANY)] * 2 + [pl.BlockSpec(memory_space=pltpu.VMEM)] * 4,
        out_specs=(pl.BlockSpec(memory_space=pltpu.VMEM),) * 2,
        scratch_shapes=[
            pltpu.VMEM((slab_depth, height + 16, cols), F32),
            pltpu.VMEM((stacks, slab_depth * padded_rows, cols), BF16),
            pltpu.VMEM((stacks, slab_depth * padded_rows, cols), BF16),
            pltpu.VMEM((slab_depth * padded_rows + 8, cols), F32),
            pltpu.VMEM((2, slab_depth * HALF, height), F32),
            pltpu.VMEM((2, stacks, slab_depth * HALF, height), F32),
            pltpu.VMEM((height + 16, LANE), F32),
            pltpu.VMEM((LANE, LANE), F32),
            pltpu.VMEM((LANE, 2 * LANE), BF16),
            pltpu.VMEM((depth + 2 * HALF, rows * chans, cols), F32),
            pltpu.VMEM((depth, rows, cols), jnp.int32),
            pltpu.VMEM((cols // LANE, depth, rows, LANE), F32),
            pltpu.VMEM((cols // LANE, depth, rows, LANE), F32),
            pltpu.VMEM((highs * chans + 16, LO), F32),
            pltpu.SemaphoreType.DMA((2,)),
            pltpu.SemaphoreType.DMA((stacks,)),
            pltpu.SemaphoreType.DMA((stacks,)),
            pltpu.SemaphoreType.DMA((2, stacks)),
            pltpu.SemaphoreType.DMA((2, stacks)),
        ],
        compiler_params=pltpu.CompilerParams(
            collective_id=0, has_side_effects=True, vmem_limit_bytes=48 << 20
        ),
        name="pencil",
    )(slab_image, fragment_ids, width_taps.T, height_taps.T, depth_taps.T, fragment_owner.reshape(1, fragments))
    gathered = pl.pallas_call(
        gather_kernel,
        out_shape=jax.ShapeDtypeStruct((lanes,) + pay.shape, F32),
        in_specs=[pl.BlockSpec(memory_space=pltpu.VMEM)],
        out_specs=pl.BlockSpec(memory_space=pltpu.VMEM),
        scratch_shapes=[pltpu.SemaphoreType.DMA((lanes,)), pltpu.SemaphoreType.DMA((lanes,))],
        compiler_params=pltpu.CompilerParams(
            collective_id=1, has_side_effects=True, vmem_limit_bytes=16 << 20
        ),
        name="gather",
    )(pay)
    fine = fine_offsets.shape[1]
    pseudo = float(fragment_ids.size // fine)
    centroids = pl.pallas_call(
        functools.partial(refine_kernel, pseudo),
        out_shape=jax.ShapeDtypeStruct((chans, fine), F32),
        in_specs=[pl.BlockSpec(memory_space=pltpu.VMEM)] * 4,
        out_specs=pl.BlockSpec(memory_space=pltpu.VMEM),
        scratch_shapes=[
            pltpu.VMEM((lanes, 9 * chans, fragments), BF16),
            pltpu.VMEM((lanes, 1, fragments), F32),
        ],
        compiler_params=pltpu.CompilerParams(vmem_limit_bytes=48 << 20),
        name="refine",
    )(gathered, coarse_centroids, parent_map.reshape(1, fine), fine_offsets)
    return (means, centroids)


def solution(mesh):
    placed = (
        P("gz", None, "xy"),
        P(),
        P(),
        P(),
        P(None, "gz", "xy"),
        P(("gz", "xy"), None),
        P(None, ("gz", "xy")),
        P(("gz", "xy")),
        P(None, ("gz", "xy")),
    )
    return jax.shard_map(
        shards,
        mesh=mesh,
        in_specs=placed,
        out_specs=(P(None, ("gz", "xy")), P(None, ("gz", "xy"))),
        check_vma=False,
    )
```

```python
import functools

import jax
import jax.numpy as jnp
from jax import lax
from jax.experimental import pallas as pl
from jax.experimental.pallas import tpu as pltpu
from jax.sharding import PartitionSpec as P

TAPS = 5
HALF = TAPS // 2
ITERS = 3
HIGH = lax.Precision.HIGHEST
sharpness = 2.0
LO = 128
F32 = jnp.float32
BF16 = jnp.bfloat16


MESH = pl.DeviceIdType.MESH
LANE = 128
PART = 16
FEW = 32
CAP = 512
SPREAD = 240.0


def encode(x):
    return jnp.exp2((x - 0.5) * SPREAD)


def decode(x):
    return jnp.log2(x) * (1.0 / SPREAD) + 0.5


def pencil_kernel(
    img, ids, wide_in, tall_in, deep_in, owner_in, gathered, means_ref,
    image, blocks, came, pack, strips, edges, halo, turned, square, filt,
    planar, whole_ids, highs_f, lows_f, thirds_f, fourths_f, acc, counts, wide, tall, deep, owner, slots, pay,
    load, send, recv, side_send, side_recv, pay_send, pay_recv,
):
    here = lax.axis_index("gz")
    lane = lax.axis_index("xy")
    stacks = lax.axis_size("gz")
    lanes = lax.axis_size("xy")
    thick, height, cols = img.shape
    depth, rows, _ = ids.shape
    padded = rows + TAPS - 1
    size = thick * padded
    wide_rows = thick * HALF
    chans, fragments = means_ref.shape
    highs = fragments // LO

    barrier = pltpu.get_barrier_semaphore()

    def greet(d, carry):
        j = lax.rem(here + d, stacks)

        @pl.when(d > 0)
        def _():
            pl.semaphore_signal(barrier, inc=1, device_id=(j, lane), device_id_type=MESH)

        @pl.when(lane > 0)
        def _():
            pl.semaphore_signal(barrier, inc=1, device_id=(j, lane - 1), device_id_type=MESH)

        @pl.when(lane < lanes - 1)
        def _():
            pl.semaphore_signal(barrier, inc=1, device_id=(j, lane + 1), device_id_type=MESH)

        return carry

    img_load = pltpu.make_async_copy(img, image.at[:, pl.ds(8, height), :], load.at[0])
    img_load.start()
    lax.fori_loop(0, stacks, greet, 0)

    def greet_lane(d, carry):
        t = lax.rem(lane + d, lanes)

        @pl.when(jnp.logical_or(t > lane + 1, t < lane - 1))
        def _():
            pl.semaphore_signal(barrier, inc=1, device_id=(here, t), device_id_type=MESH)

        return carry

    lax.fori_loop(1, lanes, greet_lane, 0)
    loads = [
        pltpu.make_async_copy(source, target, load.at[i + 1])
        for i, (source, target) in enumerate(
            ((ids, whole_ids), (wide_in, wide), (tall_in, tall), (deep_in, deep), (owner_in, owner))
        )
    ]
    for part in loads:
        part.start()

    @pl.when(lane == 0)
    def _():
        halo[0] = jnp.zeros(halo.shape[1:], F32)

    @pl.when(lane == lanes - 1)
    def _():
        halo[1] = jnp.zeros(halo.shape[1:], F32)

    blank = encode(jnp.zeros((thick, 8, cols), F32))
    image[:, :8, :] = blank
    image[:, 8 + height :, :] = blank
    turned[:8, :] = jnp.zeros((8, LANE), F32)
    turned[8 + height :, :] = jnp.zeros((8, LANE), F32)
    square[...] = jnp.zeros(square.shape, F32)
    img_load.wait()
    spot = lax.broadcasted_iota(jnp.int32, (LANE, LANE), 1)
    for y in range(0, height, LANE):
        mixed = jnp.zeros((LANE, LANE), F32)
        for z in range(thick):
            first = image[z, 8 + y : 8 + y + LANE, :LANE]
            last = image[z, 8 + y : 8 + y + LANE, cols - LANE :]
            at = z * HALF
            mixed = jnp.where((spot >= at) & (spot < at + HALF), pltpu.roll(last, (at + HALF) % LANE, 1), mixed)
            at = wide_rows + z * HALF
            mixed = jnp.where((spot >= at) & (spot < at + HALF), pltpu.roll(first, at, 1), mixed)
        both = jnp.transpose(mixed)
        edges[0, :, y : y + LANE] = both[:wide_rows]
        edges[1, :, y : y + LANE] = both[wide_rows : 2 * wide_rows]

    def code(i, carry):
        at = pl.ds(pl.multiple_of(8 + i * 32, 8), 32)
        for z in range(thick):
            image[z, at, :] = encode(image[z, at, :])
        return carry

    lax.fori_loop(0, height // 32, code, 0)

    def main_copy(j, source):
        return pltpu.make_async_remote_copy(
            src_ref=blocks.at[j],
            dst_ref=came.at[source],
            send_sem=send.at[j],
            recv_sem=recv.at[source],
            device_id=(j, lane),
            device_id_type=MESH,
        )

    def side_copy(side, j, source, target):
        return pltpu.make_async_remote_copy(
            src_ref=edges.at[side],
            dst_ref=halo.at[side, source],
            send_sem=side_send.at[side, j],
            recv_sem=side_recv.at[side, source],
            device_id=(j, target),
            device_id_type=MESH,
        )

    sides = lax.div(lane + lanes - 1, lanes) + lax.div(2 * lanes - 2 - lane, lanes)
    pl.semaphore_wait(barrier, stacks - 1 + stacks * sides + lanes - 1 - sides)

    def build(j):
        for z in range(thick):
            view = image.at[z, pl.ds(pl.multiple_of(j * rows, 8), rows + 16), :]
            pack[z * padded : (z + 1) * padded, :] = view[8 - HALF : 8 - HALF + padded, :]
        blocks[j] = pack[...].astype(BF16)

    def side_start(j):
        @pl.when(lane < lanes - 1)
        def _():
            side_copy(0, j, here, lane + 1).start()

        @pl.when(lane > 0)
        def _():
            side_copy(1, j, here, lane - 1).start()

    half = stacks // 2
    upper = (2 * here) // stacks
    rank = here - upper * half

    def near(d):
        return upper * half + lax.rem(rank + d, half)

    def far(d):
        return (1 - upper) * half + lax.rem(rank + d, half)

    def start_near(d, carry):
        j = near(d)
        build(j)

        @pl.when(d > 0)
        def _():
            main_copy(j, here).start()

        side_start(j)
        return carry

    lax.fori_loop(0, half, start_near, 0)
    came[here] = blocks[here]

    def build_far(d, carry):
        build(far(d))
        return carry

    lax.fori_loop(0, half, build_far, 0)

    for e in range(HALF):
        planar[e] = jnp.zeros(planar.shape[1:], F32)
        planar[depth + HALF + e] = jnp.zeros(planar.shape[1:], F32)
    acc[...] = jnp.zeros(acc.shape, F32)
    for part in loads:
        part.wait()

    for kind, part in enumerate((wide, tall, deep)):
        square[kind * 8 : kind * 8 + TAPS, :chans] = part[...]
    flipped = jnp.transpose(square[...])
    tap = [
        jnp.broadcast_to(flipped[:chans, k * 8 + i : k * 8 + i + 1], (chans, LANE))
        for k in range(3)
        for i in range(TAPS)
    ]
    group = TAPS * PART
    half_rows = PART // 2
    for t in range(2):
        line = lax.broadcasted_iota(jnp.int32, (chans, LANE), 1) + t * LANE
        shift_of = line % group // PART
        row_of = line % PART
        kind_of = line // group
        across = jnp.zeros((chans, LANE), F32)
        for b in range(TAPS):
            across = jnp.where((shift_of == b) & (kind_of < 3), tap[b], across)
        for odd in range(2):
            for y in range(half_rows):
                down = jnp.zeros((chans, LANE), F32)
                for a in range(TAPS):
                    down = jnp.where(row_of == y + a + 4 * odd, tap[TAPS + a], down)
                both = across * down
                high = both.astype(BF16)
                low = (both - high.astype(F32)).astype(BF16)
                filt[odd, y * chans : (y + 1) * chans, t * LANE : (t + 1) * LANE] = jnp.where(
                    kind_of == 1, low.astype(F32), high.astype(F32)
                ).astype(BF16)

    strip_spot = lax.broadcasted_iota(jnp.int32, (24, LANE), 1)
    spots = lax.broadcasted_iota(jnp.int32, (size, LANE), 1)

    def shifted(tiles, shift):
        if shift == 0:
            return jnp.concatenate(tiles[1:], axis=1)
        moved = [pltpu.roll(t, (-shift) % LANE, 1) for t in tiles]
        if shift < 0:
            out = [jnp.where(spots < -shift, moved[t - 1], moved[t]) for t in range(1, len(tiles))]
        else:
            out = [
                jnp.where(spots >= LANE - shift, moved[(t + 1) % len(tiles)], moved[t])
                for t in range(1, len(tiles))
            ]
        return jnp.concatenate(out, axis=1)

    def plane(slab):
        for y in range(0, height, LANE):
            turned[8 + y : 8 + y + LANE, :] = jnp.transpose(
                jnp.concatenate(
                    [halo[0, slab, :, y : y + LANE], halo[1, slab, :, y : y + LANE],
                     jnp.zeros((LANE - 2 * wide_rows, LANE), F32)],
                    axis=0,
                )
            )
        strip = turned[pl.ds(here * rows + 8 - HALF, 24), :]
        for z in range(thick):
            left = pltpu.roll(strip, (LANE - HALF - z * HALF) % LANE, 1)
            right = pltpu.roll(strip, (LANE - wide_rows - z * HALF) % LANE, 1)
            strips[z * padded : z * padded + padded, :] = jnp.where(
                strip_spot < LANE // 2, right, left
            )[:padded]
        now = decode(came[slab].astype(F32))
        tiles = [strips[...]] + [now[:, x : x + LANE] for x in range(0, cols, LANE)]
        moved = [shifted(tiles, b - HALF) for b in range(TAPS)]
        high = [t.astype(BF16).astype(F32) for t in moved]
        low = [t - h for t, h in zip(moved, high)]
        rest = jnp.zeros((2 * LANE - 3 * group, cols), BF16)
        for z in range(thick):
            first = z * padded // 8 * 8
            odd = z * padded % 8 // 4
            for y in range(0, rows, half_rows):
                at = slice(first + y, first + y + PART)
                upper = jnp.concatenate([t[at] for t in high], axis=0).astype(BF16)
                lower = jnp.concatenate([t[at] for t in low], axis=0).astype(BF16)
                total = jnp.dot(
                    filt[odd], jnp.concatenate([upper, upper, lower, rest], axis=0),
                    preferred_element_type=F32,
                )
                planar[slab * thick + z + HALF, y * chans : (y + half_rows) * chans, :] = (
                    total.astype(BF16).astype(F32)
                )

    shift = LO.bit_length() - 1
    few = FEW.bit_length() - 1
    many = LO // FEW * highs
    code_line = lax.broadcasted_iota(jnp.int32, (max(many, FEW), LANE), 0).astype(F32).astype(BF16)
    unit = jnp.ones((max(many, FEW), LANE), BF16)
    nil = jnp.zeros((max(many, FEW), LANE), BF16)

    def wider(row, length):
        row = jnp.broadcast_to(row, (16, LANE)).astype(BF16)
        return jnp.concatenate([row] * (length // 16), axis=0)

    def sort(slab, carry):
        left, right = [], []
        for k in range(thick):
            z = slab * thick + k
            for x in range(0, cols, LANE):
                part = whole_ids[z, :, x : x + LANE]
                high = part >> shift
                low = part & (LO - 1)
                highs_f[x // LANE, z] = high.astype(F32)
                lows_f[x // LANE, z] = low.astype(F32)
                thirds_f[x // LANE, z] = ((low >> few) * highs + high).astype(F32)
                fourths_f[x // LANE, z] = (low & (FEW - 1)).astype(F32)
        for k in range(thick):
            z = slab * thick + k
            for y in range(rows):
                for x in range(0, cols, LANE):
                    row = wider(thirds_f[x // LANE, z, pl.ds(y, 1), :], many)
                    left.append(jnp.where(row == code_line[:many], unit[:many], nil[:many]))
                    row = wider(fourths_f[x // LANE, z, pl.ds(y, 1), :], FEW)
                    right.append(jnp.where(row == code_line[:FEW], unit[:FEW], nil[:FEW]))
        counts[...] += lax.dot_general(
            jnp.concatenate(left, axis=1), jnp.concatenate(right, axis=1),
            (((1,), (1,)), ((), ())), preferred_element_type=F32,
        )
        return carry

    counts[...] = jnp.zeros(counts.shape, F32)
    lax.fori_loop(0, half, sort, 0)
    taken = jnp.concatenate([(owner[...] == t).astype(F32) for t in range(lanes)], axis=0)
    lines = lanes * highs
    over = lax.broadcasted_iota(jnp.int32, (LANE, LANE), 0)
    under = lax.broadcasted_iota(jnp.int32, (LANE, LANE), 1)
    within = jnp.dot(
        taken.astype(BF16), (over < under).astype(F32).astype(BF16), preferred_element_type=F32
    )
    summed = jnp.dot(taken.astype(BF16), jnp.ones((LANE, LANE), BF16), preferred_element_type=F32)
    over = lax.broadcasted_iota(jnp.int32, (lines, lines), 0)
    under = lax.broadcasted_iota(jnp.int32, (lines, lines), 1)
    before = jnp.logical_and(over // highs == under // highs, under < over).astype(F32).astype(BF16)
    within = within + jnp.dot(before, summed.astype(BF16), preferred_element_type=F32)
    slots[...] = jnp.where(taken > 0.5, within, -1.0)

    def start_far(d, carry):
        @pl.when(d > 0)
        def _():
            main_copy(near(d), here).wait_send()

        return carry

    lax.fori_loop(0, half, start_far, 0)

    def send_far(d, carry):
        main_copy(far(d), here).start()
        side_start(far(d))
        return carry

    lax.fori_loop(0, half, send_far, 0)
    lax.fori_loop(half, stacks, sort, 0)

    low_line = lax.broadcasted_iota(jnp.int32, (LO, LANE), 0).astype(F32).astype(BF16)
    high_line = (lax.broadcasted_iota(jnp.int32, (highs * chans, LANE), 0) // chans).astype(F32).astype(BF16)
    one = jnp.ones((LO, LANE), BF16)
    zero = jnp.zeros((LO, LANE), BF16)
    none = jnp.zeros((highs * chans, LANE), BF16)

    def count(z):
        left, right = [], []
        for y in range(rows):
            for x in range(0, cols, LANE):
                at = slice(y * chans, (y + 1) * chans)
                total = tap[2 * TAPS] * planar[z, at, x : x + LANE]
                for e in range(1, TAPS):
                    total = total + tap[2 * TAPS + e] * planar[z + e, at, x : x + LANE]
                feat = jnp.tanh(total).astype(BF16)
                high = highs_f[x // LANE, z, pl.ds(y, 1), :]
                low = lows_f[x // LANE, z, pl.ds(y, 1), :]
                left.append(jnp.where(
                    wider(high, highs * chans) == high_line,
                    jnp.concatenate([feat] * highs, axis=0), none,
                ))
                right.append(jnp.where(wider(low, LO) == low_line, one, zero))
        return left, right

    def tally(slab):
        left, right = [], []
        for z in range(thick):
            parts = count(slab * thick + z)
            left += parts[0]
            right += parts[1]
        acc[...] += lax.dot_general(
            jnp.concatenate(left, axis=1), jnp.concatenate(right, axis=1),
            (((1,), (1,)), ((), ())), preferred_element_type=F32,
        )

    def arrive(slab):
        @pl.when(slab != here)
        def _():
            main_copy(slab, slab).wait_recv()

        @pl.when(lane < lanes - 1)
        def _():
            side_copy(1, slab, slab, lane + 1).wait_recv()

        @pl.when(lane > 0)
        def _():
            side_copy(0, slab, slab, lane - 1).wait_recv()

    def place(i):
        return upper * (stacks - 1) + (1 - 2 * upper) * i

    def prepare(i, carry):
        arrive(place(i))
        plane(place(i))
        return carry

    lax.fori_loop(0, 2, prepare, 0)

    def work(i, carry):
        arrive(place(i + 2))
        tally(place(i))
        plane(place(i + 2))
        return carry

    lax.fori_loop(0, stacks - 2, work, 0)

    def close(i, carry):
        tally(place(i))
        return carry

    lax.fori_loop(stacks - 2, stacks, close, 0)

    def drain(d, carry):
        main_copy(far(d), here).wait_send()
        return carry

    lax.fori_loop(0, half, drain, 0)

    def finish(d, carry):
        j = lax.rem(here + d, stacks)

        @pl.when(lane < lanes - 1)
        def _():
            side_copy(0, j, here, lane + 1).wait_send()

        @pl.when(lane > 0)
        def _():
            side_copy(1, j, here, lane - 1).wait_send()

        return carry

    lax.fori_loop(0, stacks, finish, 0)
    every = jnp.concatenate(
        [counts[q * highs : (q + 1) * highs, :] for q in range(LO // FEW)], axis=1
    )
    kind = lax.broadcasted_iota(jnp.int32, (chans, LANE), 0)
    left = []
    for h in range(highs):
        count_row = every[h : h + 1, :]
        mean = acc[h * chans : (h + 1) * chans, :] / count_row
        means_ref[:, h * LO : (h + 1) * LO] = mean
        tally_parts = [jnp.broadcast_to(p.astype(F32), (chans, LANE)) for p in split3(count_row)]
        rows_of = jnp.where(kind == 0, tally_parts[0], jnp.where(kind == 1, tally_parts[1], tally_parts[2]))
        rows_of = jnp.where(kind < 3, rows_of, 0.0).astype(BF16)
        left.append(jnp.concatenate(list(split3(mean)) + [rows_of], axis=0))
    left = jnp.concatenate(left, axis=1)
    cap = pay.shape[2]
    slot_line = lax.broadcasted_iota(jnp.int32, (cap // 2, LANE), 0).astype(F32).astype(BF16)
    full = jnp.ones((cap // 2, LANE), BF16)
    bare = jnp.zeros((cap // 2, LANE), BF16)

    def pay_copy(target, source):
        return pltpu.make_async_remote_copy(
            src_ref=pay.at[target],
            dst_ref=gathered.at[source],
            send_sem=pay_send.at[target],
            recv_sem=pay_recv.at[source],
            device_id=(here, target),
            device_id_type=MESH,
        )

    def share(d, carry):
        t = lax.rem(lane + d, lanes)
        right = []
        for h in range(highs):
            row = slots[pl.ds(t * highs + h, 1), :]
            right.append(jnp.concatenate(
                [jnp.where(wider(row - float(p), cap // 2) == slot_line, full, bare)
                 for p in (0, cap // 2)],
                axis=0,
            ))
        out = lax.dot_general(
            left, jnp.concatenate(right, axis=1), (((1,), (1,)), ((), ())),
            preferred_element_type=F32,
        )
        pay[t, :chans, :] = out[:chans] + out[chans : 2 * chans] + out[2 * chans : 3 * chans]
        weight = out[3 * chans : 3 * chans + 1] + out[3 * chans + 1 : 3 * chans + 2] + out[3 * chans + 2 : 3 * chans + 3]
        pay[t, chans:, :] = jnp.broadcast_to(weight, (pay.shape[1] - chans, cap))

        @pl.when(d < lanes)
        def _():
            pay_copy(t, lane).start()

        return carry

    lax.fori_loop(1, lanes + 1, share, 0)
    gathered[lane] = pay[lane]

    def settle(d, carry):
        t = lax.rem(lane + d, lanes)
        pay_copy(t, lane).wait_send()
        pay_copy(t, t).wait_recv()
        return carry

    lax.fori_loop(1, lanes, settle, 0)


def split3(x):
    high = x.astype(BF16)
    rest = x - high.astype(F32)
    mid = rest.astype(BF16)
    low = (rest - mid.astype(F32)).astype(BF16)
    return high, mid, low


def refine_kernel(
    pseudo, pay_in, means, coarse_in, parent_in, offsets_in, means_ref, out_ref,
    pay, coarse, parent, offsets, factors, norms, load,
):
    loads = [
        pltpu.make_async_copy(source, target, load.at[i])
        for i, (source, target) in enumerate(
            ((pay_in, pay), (coarse_in, coarse), (parent_in, parent), (offsets_in, offsets), (means, means_ref))
        )
    ]
    for part in loads:
        part.start()
    for part in loads[:-1]:
        part.wait()
    sources, _, fragments = pay.shape
    chans = out_ref.shape[0]
    coarse_count = coarse.shape[1]
    fine = out_ref.shape[1]
    select = (
        jnp.broadcast_to(parent[...], (coarse_count, fine))
        == lax.broadcasted_iota(jnp.int32, (coarse_count, fine), 0)
    ).astype(F32)
    cents = jnp.dot(coarse[...], select, precision=HIGH, preferred_element_type=F32) + offsets[...]

    def prepare(s, carry):
        frags = pay[s, :chans, :]
        fh, fm, fl = split3(-2.0 * frags)
        ones = jnp.ones((3 * chans, fragments), BF16)
        factors[s] = jnp.concatenate([fh, fm, fh, fl, fm, fh, ones], axis=0)
        norms[s] = jnp.sum(frags * frags, axis=0, keepdims=True)
        return carry

    lax.fori_loop(0, sources, prepare, 0)

    def iterate(step, cents):
        ch, cm, cl = split3(cents)
        sh, sm, sl = split3(cents * cents)
        keys = jnp.concatenate([ch, ch, cm, ch, cm, cl, sh, sm, sl], axis=0)

        def visit(s, total):
            distance = norms[s] + lax.dot_general(
                keys, factors[s], (((0,), (0,)), ((), ())), preferred_element_type=F32
            )
            scores = -sharpness * distance
            top = jnp.max(scores, axis=0, keepdims=True)
            expo = jnp.exp(scores - top)
            scale = pay[s, chans : chans + 1, :] / jnp.sum(expo, axis=0, keepdims=True)
            scale = jnp.broadcast_to(scale, (chans, fragments))
            gh, gm, gl = split3(jnp.concatenate([pay[s, :chans, :] * scale, scale], axis=0))
            eh = expo.astype(BF16)
            em = (expo - eh.astype(F32)).astype(BF16)
            dims = (((1,), (1,)), ((), ()))
            first = lax.dot_general(
                jnp.concatenate([gh, gm, gl], axis=0), eh, dims, preferred_element_type=F32
            )
            second = lax.dot_general(
                jnp.concatenate([gh, gm], axis=0), em, dims, preferred_element_type=F32
            )
            size = 2 * chans
            return (
                total
                + (first[2 * size :] + second[size:])
                + (first[size : 2 * size] + second[:size])
                + first[:size]
            )

        total = lax.fori_loop(
            0, sources, visit, jnp.zeros((2 * chans, fine), F32), unroll=4
        )
        return (total[:chans] + pseudo * cents) / (total[chans:] + pseudo)

    out_ref[...] = lax.fori_loop(0, ITERS, iterate, cents)
    loads[-1].wait()


def shards(
    slab_image,
    width_taps,
    height_taps,
    depth_taps,
    fragment_ids,
    fragment_owner,
    coarse_centroids,
    parent_map,
    fine_offsets,
):
    chans = width_taps.shape[0]
    depth, rows, cols = fragment_ids.shape
    fragments = fragment_owner.shape[0]
    lanes = lax.axis_size("xy")
    stacks = lax.axis_size("gz")
    padded_rows = rows + TAPS - 1
    slab_depth, height, _ = slab_image.shape
    highs = fragments // LO
    assert highs <= 16
    cap = min(CAP, fragments)
    gathered, means = pl.pallas_call(
        pencil_kernel,
        out_shape=(
            jax.ShapeDtypeStruct((lanes, chans + 8, cap), F32),
            jax.ShapeDtypeStruct((chans, fragments), F32),
        ),
        in_specs=[pl.BlockSpec(memory_space=pltpu.HBM)] * 6,
        out_specs=(pl.BlockSpec(memory_space=pltpu.VMEM),) * 2,
        scratch_shapes=[
            pltpu.VMEM((slab_depth, height + 16, cols), F32),
            pltpu.VMEM((stacks, slab_depth * padded_rows, cols), BF16),
            pltpu.VMEM((stacks, slab_depth * padded_rows, cols), BF16),
            pltpu.VMEM((slab_depth * padded_rows, cols), F32),
            pltpu.VMEM((slab_depth * padded_rows, LANE), F32),
            pltpu.VMEM((2, slab_depth * HALF, height), F32),
            pltpu.VMEM((2, stacks, slab_depth * HALF, height), F32),
            pltpu.VMEM((height + 16, LANE), F32),
            pltpu.VMEM((LANE, LANE), F32),
            pltpu.VMEM((2, LANE, 2 * LANE), BF16),
            pltpu.VMEM((depth + 2 * HALF, rows * chans, cols), F32),
            pltpu.VMEM((depth, rows, cols), jnp.int32),
            pltpu.VMEM((cols // LANE, depth, rows, LANE), F32),
            pltpu.VMEM((cols // LANE, depth, rows, LANE), F32),
            pltpu.VMEM((cols // LANE, depth, rows, LANE), F32),
            pltpu.VMEM((cols // LANE, depth, rows, LANE), F32),
            pltpu.VMEM((highs * chans, LO), F32),
            pltpu.VMEM((LO // FEW * highs, FEW), F32),
            pltpu.VMEM((TAPS, chans), F32),
            pltpu.VMEM((TAPS, chans), F32),
            pltpu.VMEM((TAPS, chans), F32),
            pltpu.VMEM((highs, LANE), jnp.int32),
            pltpu.VMEM((lanes * highs, LANE), F32),
            pltpu.VMEM((lanes, chans + 8, cap), F32),
            pltpu.SemaphoreType.DMA((6,)),
            pltpu.SemaphoreType.DMA((stacks,)),
            pltpu.SemaphoreType.DMA((stacks,)),
            pltpu.SemaphoreType.DMA((2, stacks)),
            pltpu.SemaphoreType.DMA((2, stacks)),
            pltpu.SemaphoreType.DMA((lanes,)),
            pltpu.SemaphoreType.DMA((lanes,)),
        ],
        compiler_params=pltpu.CompilerParams(
            collective_id=0, has_side_effects=True, vmem_limit_bytes=60 << 20
        ),
        name="pencil",
    )(slab_image, fragment_ids, width_taps.T, height_taps.T, depth_taps.T, fragment_owner.reshape(highs, LANE))
    fine = fine_offsets.shape[1]
    pseudo = float(fragment_ids.size // fine)
    return pl.pallas_call(
        functools.partial(refine_kernel, pseudo),
        out_shape=(
            jax.ShapeDtypeStruct((chans, fragments), F32),
            jax.ShapeDtypeStruct((chans, fine), F32),
        ),
        in_specs=[pl.BlockSpec(memory_space=pltpu.HBM)] * 5,
        out_specs=(pl.BlockSpec(memory_space=pltpu.HBM), pl.BlockSpec(memory_space=pltpu.VMEM)),
        scratch_shapes=[
            pltpu.VMEM((lanes, chans + 8, cap), F32),
            pltpu.VMEM(coarse_centroids.shape, F32),
            pltpu.VMEM((1, fine), jnp.int32),
            pltpu.VMEM((chans, fine), F32),
            pltpu.VMEM((lanes, 9 * chans, cap), BF16),
            pltpu.VMEM((lanes, 1, cap), F32),
            pltpu.SemaphoreType.DMA((5,)),
        ],
        compiler_params=pltpu.CompilerParams(vmem_limit_bytes=60 << 20),
        name="refine",
    )(gathered, means, coarse_centroids, parent_map.reshape(1, fine), fine_offsets)


def solution(mesh):
    placed = (
        P("gz", None, "xy"),
        P(),
        P(),
        P(),
        P(None, "gz", "xy"),
        P(("gz", "xy"), None),
        P(None, ("gz", "xy")),
        P(("gz", "xy")),
        P(None, ("gz", "xy")),
    )
    return jax.shard_map(
        shards,
        mesh=mesh,
        in_specs=placed,
        out_specs=(P(None, ("gz", "xy")), P(None, ("gz", "xy"))),
        check_vma=False,
    )
```

```python
import functools

import jax
import jax.numpy as jnp
from jax import lax
from jax.experimental import pallas as pl
from jax.experimental.pallas import tpu as pltpu
from jax.sharding import PartitionSpec as P

TAPS = 5
HALF = TAPS // 2
ITERS = 3
HIGH = lax.Precision.HIGHEST
sharpness = 2.0
LO = 128
F32 = jnp.float32
BF16 = jnp.bfloat16


MESH = pl.DeviceIdType.MESH
LANE = 128
PART = 16
FEW = 32
CAP = 512
SPREAD = 240.0


def encode(x):
    return jnp.exp2((x - 0.5) * SPREAD)


def decode(x):
    return jnp.log2(x) * (1.0 / SPREAD) + 0.5


def pencil_kernel(
    img, ids, wide_in, tall_in, deep_in, owner_in, gathered, means_to,
    image, blocks, came, pack, strips, edges, halo, turned, square, filt,
    planar, whole_ids, highs_f, lows_f, thirds_f, fourths_f, acc, counts, wide, tall, deep, owner, slots, pay, means_ref,
    load, send, recv, side_send, side_recv, pay_send, pay_recv,
):
    here = lax.axis_index("gz")
    lane = lax.axis_index("xy")
    stacks = lax.axis_size("gz")
    lanes = lax.axis_size("xy")
    thick, height, cols = img.shape
    depth, rows, _ = ids.shape
    padded = rows + TAPS - 1
    size = thick * padded
    wide_rows = thick * HALF
    chans, fragments = means_ref.shape
    highs = fragments // LO
    means_out = pltpu.make_async_copy(means_ref, means_to, load.at[1])

    barrier = pltpu.get_barrier_semaphore()

    def greet(d, carry):
        j = lax.rem(here + d, stacks)

        @pl.when(d > 0)
        def _():
            pl.semaphore_signal(barrier, inc=1, device_id=(j, lane), device_id_type=MESH)

        @pl.when(lane > 0)
        def _():
            pl.semaphore_signal(barrier, inc=1, device_id=(j, lane - 1), device_id_type=MESH)

        @pl.when(lane < lanes - 1)
        def _():
            pl.semaphore_signal(barrier, inc=1, device_id=(j, lane + 1), device_id_type=MESH)

        return carry

    img_load = pltpu.make_async_copy(img, image.at[:, pl.ds(8, height), :], load.at[0])
    img_load.start()
    lax.fori_loop(0, stacks, greet, 0)

    def greet_lane(d, carry):
        t = lax.rem(lane + d, lanes)

        @pl.when(jnp.logical_or(t > lane + 1, t < lane - 1))
        def _():
            pl.semaphore_signal(barrier, inc=1, device_id=(here, t), device_id_type=MESH)

        return carry

    lax.fori_loop(1, lanes, greet_lane, 0)
    loads = [
        pltpu.make_async_copy(source, target, load.at[i + 1])
        for i, (source, target) in enumerate(
            ((ids, whole_ids), (wide_in, wide), (tall_in, tall), (deep_in, deep), (owner_in, owner))
        )
    ]
    for part in loads:
        part.start()

    @pl.when(lane == 0)
    def _():
        halo[0] = jnp.zeros(halo.shape[1:], F32)

    @pl.when(lane == lanes - 1)
    def _():
        halo[1] = jnp.zeros(halo.shape[1:], F32)

    blank = encode(jnp.zeros((thick, 8, cols), F32))
    image[:, :8, :] = blank
    image[:, 8 + height :, :] = blank
    turned[:8, :] = jnp.zeros((8, LANE), F32)
    turned[8 + height :, :] = jnp.zeros((8, LANE), F32)
    square[...] = jnp.zeros(square.shape, F32)
    img_load.wait()
    spot = lax.broadcasted_iota(jnp.int32, (LANE, LANE), 1)
    for y in range(0, height, LANE):
        mixed = jnp.zeros((LANE, LANE), F32)
        for z in range(thick):
            first = image[z, 8 + y : 8 + y + LANE, :LANE]
            last = image[z, 8 + y : 8 + y + LANE, cols - LANE :]
            at = z * HALF
            mixed = jnp.where((spot >= at) & (spot < at + HALF), pltpu.roll(last, (at + HALF) % LANE, 1), mixed)
            at = wide_rows + z * HALF
            mixed = jnp.where((spot >= at) & (spot < at + HALF), pltpu.roll(first, at, 1), mixed)
        both = jnp.transpose(mixed)
        edges[0, :, y : y + LANE] = both[:wide_rows]
        edges[1, :, y : y + LANE] = both[wide_rows : 2 * wide_rows]

    def code(i, carry):
        at = pl.ds(pl.multiple_of(8 + i * 32, 8), 32)
        for z in range(thick):
            image[z, at, :] = encode(image[z, at, :])
        return carry

    lax.fori_loop(0, height // 32, code, 0)

    def main_copy(j, source):
        return pltpu.make_async_remote_copy(
            src_ref=blocks.at[j],
            dst_ref=came.at[source],
            send_sem=send.at[j],
            recv_sem=recv.at[source],
            device_id=(j, lane),
            device_id_type=MESH,
        )

    def side_copy(side, j, source, target):
        return pltpu.make_async_remote_copy(
            src_ref=edges.at[side],
            dst_ref=halo.at[side, source],
            send_sem=side_send.at[side, j],
            recv_sem=side_recv.at[side, source],
            device_id=(j, target),
            device_id_type=MESH,
        )

    sides = lax.div(lane + lanes - 1, lanes) + lax.div(2 * lanes - 2 - lane, lanes)
    pl.semaphore_wait(barrier, stacks - 1 + stacks * sides + lanes - 1 - sides)

    def build(j):
        for z in range(thick):
            view = image.at[z, pl.ds(pl.multiple_of(j * rows, 8), rows + 16), :]
            pack[z * padded : (z + 1) * padded, :] = view[8 - HALF : 8 - HALF + padded, :]
        blocks[j] = pack[...].astype(BF16)

    def side_start(j):
        @pl.when(lane < lanes - 1)
        def _():
            side_copy(0, j, here, lane + 1).start()

        @pl.when(lane > 0)
        def _():
            side_copy(1, j, here, lane - 1).start()

    half = stacks // 2
    upper = (2 * here) // stacks
    rank = here - upper * half

    def near(d):
        pair = lax.rem(rank // 2 + d // 2, half // 2)
        return upper * half + 2 * pair + lax.rem(rank + d, 2)

    def far(d):
        return (1 - upper) * half + lax.rem(rank + d, half)

    def start_near(d, carry):
        j = near(d)
        build(j)

        @pl.when(d > 0)
        def _():
            main_copy(j, here).start()

        side_start(j)
        return carry

    lax.fori_loop(0, half, start_near, 0)
    came[here] = blocks[here]

    def build_far(d, carry):
        build(far(d))
        return carry

    lax.fori_loop(0, half, build_far, 0)

    for e in range(HALF):
        planar[e] = jnp.zeros(planar.shape[1:], F32)
        planar[depth + HALF + e] = jnp.zeros(planar.shape[1:], F32)
    acc[...] = jnp.zeros(acc.shape, F32)
    for part in loads:
        part.wait()

    for kind, part in enumerate((wide, tall, deep)):
        square[kind * 8 : kind * 8 + TAPS, :chans] = part[...]
    flipped = jnp.transpose(square[...])
    tap = [
        jnp.broadcast_to(flipped[:chans, k * 8 + i : k * 8 + i + 1], (chans, LANE))
        for k in range(3)
        for i in range(TAPS)
    ]
    group = TAPS * PART
    half_rows = PART // 2
    for t in range(2):
        line = lax.broadcasted_iota(jnp.int32, (chans, LANE), 1) + t * LANE
        shift_of = line % group // PART
        row_of = line % PART
        kind_of = line // group
        across = jnp.zeros((chans, LANE), F32)
        for b in range(TAPS):
            across = jnp.where((shift_of == b) & (kind_of < 3), tap[b], across)
        for odd in range(2):
            for y in range(half_rows):
                down = jnp.zeros((chans, LANE), F32)
                for a in range(TAPS):
                    down = jnp.where(row_of == y + a + 4 * odd, tap[TAPS + a], down)
                both = across * down
                high = both.astype(BF16)
                low = (both - high.astype(F32)).astype(BF16)
                filt[odd, y * chans : (y + 1) * chans, t * LANE : (t + 1) * LANE] = jnp.where(
                    kind_of == 1, low.astype(F32), high.astype(F32)
                ).astype(BF16)

    strip_spot = lax.broadcasted_iota(jnp.int32, (24, LANE), 1)
    spots = lax.broadcasted_iota(jnp.int32, (size, LANE), 1)

    def shifted(tiles, shift):
        if shift == 0:
            return jnp.concatenate(tiles[1:], axis=1)
        moved = [pltpu.roll(t, (-shift) % LANE, 1) for t in tiles]
        if shift < 0:
            out = [jnp.where(spots < -shift, moved[t - 1], moved[t]) for t in range(1, len(tiles))]
        else:
            out = [
                jnp.where(spots >= LANE - shift, moved[(t + 1) % len(tiles)], moved[t])
                for t in range(1, len(tiles))
            ]
        return jnp.concatenate(out, axis=1)

    def plane(slab):
        for y in range(0, height, LANE):
            turned[8 + y : 8 + y + LANE, :] = jnp.transpose(
                jnp.concatenate(
                    [halo[0, slab, :, y : y + LANE], halo[1, slab, :, y : y + LANE],
                     jnp.zeros((LANE - 2 * wide_rows, LANE), F32)],
                    axis=0,
                )
            )
        strip = turned[pl.ds(here * rows + 8 - HALF, 24), :]
        for z in range(thick):
            left = pltpu.roll(strip, (LANE - HALF - z * HALF) % LANE, 1)
            right = pltpu.roll(strip, (LANE - wide_rows - z * HALF) % LANE, 1)
            strips[z * padded : z * padded + padded, :] = jnp.where(
                strip_spot < LANE // 2, right, left
            )[:padded]
        now = decode(came[slab].astype(F32))
        tiles = [strips[...]] + [now[:, x : x + LANE] for x in range(0, cols, LANE)]
        moved = [shifted(tiles, b - HALF) for b in range(TAPS)]
        high = [t.astype(BF16).astype(F32) for t in moved]
        low = [t - h for t, h in zip(moved, high)]
        rest = jnp.zeros((2 * LANE - 3 * group, cols), BF16)
        for z in range(thick):
            first = z * padded // 8 * 8
            odd = z * padded % 8 // 4
            for y in range(0, rows, half_rows):
                at = slice(first + y, first + y + PART)
                upper = jnp.concatenate([t[at] for t in high], axis=0).astype(BF16)
                lower = jnp.concatenate([t[at] for t in low], axis=0).astype(BF16)
                total = jnp.dot(
                    filt[odd], jnp.concatenate([upper, upper, lower, rest], axis=0),
                    preferred_element_type=F32,
                )
                planar[slab * thick + z + HALF, y * chans : (y + half_rows) * chans, :] = (
                    total.astype(BF16).astype(F32)
                )

    shift = LO.bit_length() - 1
    few = FEW.bit_length() - 1
    many = LO // FEW * highs
    code_line = lax.broadcasted_iota(jnp.int32, (max(many, FEW), LANE), 0).astype(F32).astype(BF16)
    unit = jnp.ones((max(many, FEW), LANE), BF16)
    nil = jnp.zeros((max(many, FEW), LANE), BF16)

    def wider(row, length):
        row = jnp.broadcast_to(row, (16, LANE)).astype(BF16)
        return jnp.concatenate([row] * (length // 16), axis=0)

    def sort(slab, carry):
        left, right = [], []
        for k in range(2 * thick):
            z = slab * 2 * thick + k
            for x in range(0, cols, LANE):
                part = whole_ids[z, :, x : x + LANE]
                high = part >> shift
                low = part & (LO - 1)
                highs_f[x // LANE, z] = high.astype(F32)
                lows_f[x // LANE, z] = low.astype(F32)
                thirds_f[x // LANE, z] = ((low >> few) * highs + high).astype(F32)
                fourths_f[x // LANE, z] = (low & (FEW - 1)).astype(F32)
        for k in range(2 * thick):
            z = slab * 2 * thick + k
            for y in range(rows):
                for x in range(0, cols, LANE):
                    row = wider(thirds_f[x // LANE, z, pl.ds(y, 1), :], many)
                    left.append(jnp.where(row == code_line[:many], unit[:many], nil[:many]))
                    row = wider(fourths_f[x // LANE, z, pl.ds(y, 1), :], FEW)
                    right.append(jnp.where(row == code_line[:FEW], unit[:FEW], nil[:FEW]))
        counts[...] += lax.dot_general(
            jnp.concatenate(left, axis=1), jnp.concatenate(right, axis=1),
            (((1,), (1,)), ((), ())), preferred_element_type=F32,
        )
        return carry

    counts[...] = jnp.zeros(counts.shape, F32)
    def send_far(d, carry):
        main_copy(far(d), here).start()
        side_start(far(d))
        return carry

    inner = jnp.where(upper == 0, rank, half - 1 - rank) * 2 >= half

    @pl.when(inner)
    def _():
        lax.fori_loop(0, half, send_far, 0)

    lax.fori_loop(0, half // 2, sort, 0)
    taken = jnp.concatenate([(owner[...] == t).astype(F32) for t in range(lanes)], axis=0)
    lines = lanes * highs
    over = lax.broadcasted_iota(jnp.int32, (LANE, LANE), 0)
    under = lax.broadcasted_iota(jnp.int32, (LANE, LANE), 1)
    within = jnp.dot(
        taken.astype(BF16), (over < under).astype(F32).astype(BF16), preferred_element_type=F32
    )
    summed = jnp.dot(taken.astype(BF16), jnp.ones((LANE, LANE), BF16), preferred_element_type=F32)
    over = lax.broadcasted_iota(jnp.int32, (lines, lines), 0)
    under = lax.broadcasted_iota(jnp.int32, (lines, lines), 1)
    before = jnp.logical_and(over // highs == under // highs, under < over).astype(F32).astype(BF16)
    within = within + jnp.dot(before, summed.astype(BF16), preferred_element_type=F32)
    slots[...] = jnp.where(taken > 0.5, within, -1.0)

    def start_far(d, carry):
        @pl.when(d > 0)
        def _():
            main_copy(near(d), here).wait_send()

        return carry

    @pl.when(jnp.logical_not(inner))
    def _():
        lax.fori_loop(0, half, start_far, 0)
        lax.fori_loop(0, half, send_far, 0)

    lax.fori_loop(half // 2, half, sort, 0)

    @pl.when(inner)
    def _():
        lax.fori_loop(0, half, start_far, 0)


    low_line = lax.broadcasted_iota(jnp.int32, (LO, LANE), 0).astype(F32).astype(BF16)
    high_line = (lax.broadcasted_iota(jnp.int32, (highs * chans, LANE), 0) // chans).astype(F32).astype(BF16)
    one = jnp.ones((LO, LANE), BF16)
    zero = jnp.zeros((LO, LANE), BF16)
    none = jnp.zeros((highs * chans, LANE), BF16)

    def count(z):
        left, right = [], []
        for y in range(rows):
            for x in range(0, cols, LANE):
                at = slice(y * chans, (y + 1) * chans)
                total = tap[2 * TAPS] * planar[z, at, x : x + LANE]
                for e in range(1, TAPS):
                    total = total + tap[2 * TAPS + e] * planar[z + e, at, x : x + LANE]
                feat = jnp.tanh(total).astype(BF16)
                high = highs_f[x // LANE, z, pl.ds(y, 1), :]
                low = lows_f[x // LANE, z, pl.ds(y, 1), :]
                left.append(jnp.where(
                    wider(high, highs * chans) == high_line,
                    jnp.concatenate([feat] * highs, axis=0), none,
                ))
                right.append(jnp.where(wider(low, LO) == low_line, one, zero))
        return left, right

    def tally(which):
        for k in range(0, thick, 2):
            left, right = [], []
            for more in range(2):
                parts = count(lax.rem(which * thick + HALF + k + more, depth))
                left += parts[0]
                right += parts[1]
            acc[...] += lax.dot_general(
                jnp.concatenate(left, axis=1), jnp.concatenate(right, axis=1),
                (((1,), (1,)), ((), ())), preferred_element_type=F32,
            )

    def arrive(slab):
        @pl.when(slab != here)
        def _():
            main_copy(slab, slab).wait_recv()

        @pl.when(lane < lanes - 1)
        def _():
            side_copy(1, slab, slab, lane + 1).wait_recv()

        @pl.when(lane > 0)
        def _():
            side_copy(0, slab, slab, lane - 1).wait_recv()

    inmost = jnp.where(upper == 0, rank, half - 1 - rank) // 2 * 2

    def mirrored(i, top):
        return upper * top + (1 - 2 * upper) * i

    def place(i):
        i = jnp.where(i <= 1, inmost + i, jnp.where(i <= inmost + 1, inmost + 1 - i, i))
        return mirrored(i, stacks - 1)

    def unit(i):
        turn = mirrored(jnp.where(i <= inmost, inmost - i, i), stacks - 2)
        return jnp.where(i == stacks - 1, stacks - 1, turn)

    def prepare(i, carry):
        arrive(place(i))
        plane(place(i))
        return carry

    lax.fori_loop(0, 2, prepare, 0)

    def work(i, carry):
        arrive(place(i + 2))
        tally(unit(i))
        plane(place(i + 2))
        return carry

    lax.fori_loop(0, stacks - 2, work, 0)

    def close(i, carry):
        tally(unit(i))
        return carry

    lax.fori_loop(stacks - 2, stacks, close, 0)

    def drain(d, carry):
        main_copy(far(d), here).wait_send()
        return carry

    lax.fori_loop(0, half, drain, 0)

    def finish(d, carry):
        j = lax.rem(here + d, stacks)

        @pl.when(lane < lanes - 1)
        def _():
            side_copy(0, j, here, lane + 1).wait_send()

        @pl.when(lane > 0)
        def _():
            side_copy(1, j, here, lane - 1).wait_send()

        return carry

    lax.fori_loop(0, stacks, finish, 0)
    every = jnp.concatenate(
        [counts[q * highs : (q + 1) * highs, :] for q in range(LO // FEW)], axis=1
    )
    kind = lax.broadcasted_iota(jnp.int32, (chans, LANE), 0)
    left = []
    for h in range(highs):
        count_row = every[h : h + 1, :]
        mean = acc[h * chans : (h + 1) * chans, :] / count_row
        means_ref[:, h * LO : (h + 1) * LO] = mean
        tally_parts = [jnp.broadcast_to(p.astype(F32), (chans, LANE)) for p in split3(count_row)]
        rows_of = jnp.where(kind == 0, tally_parts[0], jnp.where(kind == 1, tally_parts[1], tally_parts[2]))
        rows_of = jnp.where(kind < 3, rows_of, 0.0).astype(BF16)
        left.append(jnp.concatenate(list(split3(mean)) + [rows_of], axis=0))
    means_out.start()
    left = jnp.concatenate(left, axis=1)
    cap = pay.shape[2]
    slot_line = lax.broadcasted_iota(jnp.int32, (cap // 2, LANE), 0).astype(F32).astype(BF16)
    full = jnp.ones((cap // 2, LANE), BF16)
    bare = jnp.zeros((cap // 2, LANE), BF16)

    def pay_copy(target, source):
        return pltpu.make_async_remote_copy(
            src_ref=pay.at[target],
            dst_ref=gathered.at[source],
            send_sem=pay_send.at[target],
            recv_sem=pay_recv.at[source],
            device_id=(here, target),
            device_id_type=MESH,
        )

    def share(d, carry):
        t = lax.rem(lane + d, lanes)
        right = []
        for h in range(highs):
            row = slots[pl.ds(t * highs + h, 1), :]
            right.append(jnp.concatenate(
                [jnp.where(wider(row - float(p), cap // 2) == slot_line, full, bare)
                 for p in (0, cap // 2)],
                axis=0,
            ))
        out = lax.dot_general(
            left, jnp.concatenate(right, axis=1), (((1,), (1,)), ((), ())),
            preferred_element_type=F32,
        )
        pay[t, :chans, :] = out[:chans] + out[chans : 2 * chans] + out[2 * chans : 3 * chans]
        weight = out[3 * chans : 3 * chans + 1] + out[3 * chans + 1 : 3 * chans + 2] + out[3 * chans + 2 : 3 * chans + 3]
        pay[t, chans:, :] = jnp.broadcast_to(weight, (pay.shape[1] - chans, cap))

        @pl.when(d < lanes)
        def _():
            pay_copy(t, lane).start()

        return carry

    lax.fori_loop(1, lanes + 1, share, 0)
    own_pay = pltpu.make_async_copy(pay.at[lane], gathered.at[lane], load.at[0])
    own_pay.start()
    def settle(d, carry):
        t = lax.rem(lane + d, lanes)
        pay_copy(t, lane).wait_send()
        pay_copy(t, t).wait_recv()
        return carry

    lax.fori_loop(1, lanes, settle, 0)
    own_pay.wait()
    means_out.wait()


def split3(x):
    high = x.astype(BF16)
    rest = x - high.astype(F32)
    mid = rest.astype(BF16)
    low = (rest - mid.astype(F32)).astype(BF16)
    return high, mid, low


def refine_kernel(
    pseudo, pay_in, means, coarse_in, parent_in, offsets_in, means_ref, out_ref,
    pay, coarse, parent, offsets, factors, norms, load,
):
    loads = [
        pltpu.make_async_copy(source, target, load.at[i])
        for i, (source, target) in enumerate(
            ((pay_in, pay), (coarse_in, coarse), (parent_in, parent), (offsets_in, offsets), (means, means_ref))
        )
    ]
    for part in loads:
        part.start()
    for part in loads[:-1]:
        part.wait()
    sources, _, fragments = pay.shape
    chans = out_ref.shape[0]
    coarse_count = coarse.shape[1]
    fine = out_ref.shape[1]
    select = (
        jnp.broadcast_to(parent[...], (coarse_count, fine))
        == lax.broadcasted_iota(jnp.int32, (coarse_count, fine), 0)
    ).astype(F32)
    cents = jnp.dot(coarse[...], select, precision=HIGH, preferred_element_type=F32) + offsets[...]

    def prepare(s, carry):
        frags = pay[s, :chans, :]
        fh, fm, fl = split3(2.0 * sharpness * frags)
        ones = jnp.full((3 * chans, fragments), -sharpness, BF16)
        factors[s] = jnp.concatenate([fh, fm, fh, fl, fm, fh, ones], axis=0)
        norms[s] = -sharpness * jnp.sum(frags * frags, axis=0, keepdims=True)
        return carry

    lax.fori_loop(0, sources, prepare, 0)

    def iterate(step, cents):
        ch, cm, cl = split3(cents)
        sh, sm, sl = split3(cents * cents)
        keys = jnp.concatenate([ch, ch, cm, ch, cm, cl, sh, sm, sl], axis=0)

        def visit(s, total):
            scores = norms[s] + lax.dot_general(
                keys, factors[s], (((0,), (0,)), ((), ())), preferred_element_type=F32
            )
            top = jnp.max(scores, axis=0, keepdims=True)
            expo = jnp.exp(scores - top)
            scale = pay[s, chans : chans + 1, :] / jnp.sum(expo, axis=0, keepdims=True)
            scale = jnp.broadcast_to(scale, (chans, fragments))
            gh, gm, gl = split3(jnp.concatenate([pay[s, :chans, :] * scale, scale], axis=0))
            eh = expo.astype(BF16)
            em = (expo - eh.astype(F32)).astype(BF16)
            dims = (((1,), (1,)), ((), ()))
            first = lax.dot_general(
                jnp.concatenate([gh, gm, gl], axis=0), eh, dims, preferred_element_type=F32
            )
            second = lax.dot_general(
                jnp.concatenate([gh, gm], axis=0), em, dims, preferred_element_type=F32
            )
            size = 2 * chans
            return (
                total
                + (first[2 * size :] + second[size:])
                + (first[size : 2 * size] + second[:size])
                + first[:size]
            )

        total = lax.fori_loop(
            0, sources, visit, jnp.zeros((2 * chans, fine), F32), unroll=4
        )
        return (total[:chans] + pseudo * cents) / (total[chans:] + pseudo)

    out_ref[...] = lax.fori_loop(0, ITERS, iterate, cents)
    loads[-1].wait()


def shards(
    slab_image,
    width_taps,
    height_taps,
    depth_taps,
    fragment_ids,
    fragment_owner,
    coarse_centroids,
    parent_map,
    fine_offsets,
):
    chans = width_taps.shape[0]
    depth, rows, cols = fragment_ids.shape
    fragments = fragment_owner.shape[0]
    lanes = lax.axis_size("xy")
    stacks = lax.axis_size("gz")
    padded_rows = rows + TAPS - 1
    slab_depth, height, _ = slab_image.shape
    highs = fragments // LO
    assert highs <= 16
    cap = min(CAP, fragments)
    gathered, means = pl.pallas_call(
        pencil_kernel,
        out_shape=(
            jax.ShapeDtypeStruct((lanes, chans + 8, cap), F32),
            jax.ShapeDtypeStruct((chans, fragments), F32),
        ),
        in_specs=[pl.BlockSpec(memory_space=pltpu.HBM)] * 6,
        out_specs=(pl.BlockSpec(memory_space=pltpu.HBM),) * 2,
        scratch_shapes=[
            pltpu.VMEM((slab_depth, height + 16, cols), F32),
            pltpu.VMEM((stacks, slab_depth * padded_rows, cols), BF16),
            pltpu.VMEM((stacks, slab_depth * padded_rows, cols), BF16),
            pltpu.VMEM((slab_depth * padded_rows, cols), F32),
            pltpu.VMEM((slab_depth * padded_rows, LANE), F32),
            pltpu.VMEM((2, slab_depth * HALF, height), F32),
            pltpu.VMEM((2, stacks, slab_depth * HALF, height), F32),
            pltpu.VMEM((height + 16, LANE), F32),
            pltpu.VMEM((LANE, LANE), F32),
            pltpu.VMEM((2, LANE, 2 * LANE), BF16),
            pltpu.VMEM((depth + 2 * HALF, rows * chans, cols), F32),
            pltpu.VMEM((depth, rows, cols), jnp.int32),
            pltpu.VMEM((cols // LANE, depth, rows, LANE), F32),
            pltpu.VMEM((cols // LANE, depth, rows, LANE), F32),
            pltpu.VMEM((cols // LANE, depth, rows, LANE), F32),
            pltpu.VMEM((cols // LANE, depth, rows, LANE), F32),
            pltpu.VMEM((highs * chans, LO), F32),
            pltpu.VMEM((LO // FEW * highs, FEW), F32),
            pltpu.VMEM((TAPS, chans), F32),
            pltpu.VMEM((TAPS, chans), F32),
            pltpu.VMEM((TAPS, chans), F32),
            pltpu.VMEM((highs, LANE), jnp.int32),
            pltpu.VMEM((lanes * highs, LANE), F32),
            pltpu.VMEM((lanes, chans + 8, cap), F32),
            pltpu.VMEM((chans, fragments), F32),
            pltpu.SemaphoreType.DMA((6,)),
            pltpu.SemaphoreType.DMA((stacks,)),
            pltpu.SemaphoreType.DMA((stacks,)),
            pltpu.SemaphoreType.DMA((2, stacks)),
            pltpu.SemaphoreType.DMA((2, stacks)),
            pltpu.SemaphoreType.DMA((lanes,)),
            pltpu.SemaphoreType.DMA((lanes,)),
        ],
        compiler_params=pltpu.CompilerParams(
            collective_id=0, has_side_effects=True, vmem_limit_bytes=60 << 20
        ),
        name="pencil",
    )(slab_image, fragment_ids, width_taps.T, height_taps.T, depth_taps.T, fragment_owner.reshape(highs, LANE))
    fine = fine_offsets.shape[1]
    pseudo = float(fragment_ids.size // fine)
    return pl.pallas_call(
        functools.partial(refine_kernel, pseudo),
        out_shape=(
            jax.ShapeDtypeStruct((chans, fragments), F32),
            jax.ShapeDtypeStruct((chans, fine), F32),
        ),
        in_specs=[pl.BlockSpec(memory_space=pltpu.HBM)] * 5,
        out_specs=(pl.BlockSpec(memory_space=pltpu.HBM), pl.BlockSpec(memory_space=pltpu.VMEM)),
        scratch_shapes=[
            pltpu.VMEM((lanes, chans + 8, cap), F32),
            pltpu.VMEM(coarse_centroids.shape, F32),
            pltpu.VMEM((1, fine), jnp.int32),
            pltpu.VMEM((chans, fine), F32),
            pltpu.VMEM((lanes, 9 * chans, cap), BF16),
            pltpu.VMEM((lanes, 1, cap), F32),
            pltpu.SemaphoreType.DMA((5,)),
        ],
        compiler_params=pltpu.CompilerParams(vmem_limit_bytes=60 << 20),
        name="refine",
    )(gathered, means, coarse_centroids, parent_map.reshape(1, fine), fine_offsets)


def solution(mesh):
    placed = (
        P("gz", None, "xy"),
        P(),
        P(),
        P(),
        P(None, "gz", "xy"),
        P(("gz", "xy"), None),
        P(None, ("gz", "xy")),
        P(("gz", "xy")),
        P(None, ("gz", "xy")),
    )
    return jax.shard_map(
        shards,
        mesh=mesh,
        in_specs=placed,
        out_specs=(P(None, ("gz", "xy")), P(None, ("gz", "xy"))),
        check_vma=False,
    )
```

```python
import functools

import jax
import jax.numpy as jnp
from jax import lax
from jax.experimental import pallas as pl
from jax.experimental.pallas import tpu as pltpu
from jax.sharding import PartitionSpec as P

TAPS = 5
HALF = TAPS // 2
ITERS = 3
HIGH = lax.Precision.HIGHEST
sharpness = 2.0
LO = 128
F32 = jnp.float32
BF16 = jnp.bfloat16


MESH = pl.DeviceIdType.MESH
LANE = 128
PART = 16
FEW = 32
CAP = 512
SPREAD = 240.0


def encode(x):
    return jnp.exp2((x - 0.5) * SPREAD)


def decode(x):
    return jnp.log2(x) * (1.0 / SPREAD) + 0.5


def pencil_kernel(
    img, ids, wide_in, tall_in, deep_in, owner_in, gathered, means_to,
    image, blocks, came, pack, strips, edges, halo, turned, square, filt,
    planar, whole_ids, highs_f, lows_f, thirds_f, fourths_f, acc, counts, wide, tall, deep, owner, slots, pay, means_ref,
    load, send, recv, side_send, side_recv, pay_send, pay_recv,
):
    here = lax.axis_index("gz")
    lane = lax.axis_index("xy")
    stacks = lax.axis_size("gz")
    lanes = lax.axis_size("xy")
    thick, height, cols = img.shape
    depth, rows, _ = ids.shape
    padded = rows + TAPS - 1
    size = thick * padded
    wide_rows = thick * HALF
    chans, fragments = means_ref.shape
    highs = fragments // LO
    means_out = pltpu.make_async_copy(means_ref, means_to, load.at[1])

    barrier = pltpu.get_barrier_semaphore()

    def greet(d, carry):
        j = lax.rem(here + d, stacks)

        @pl.when(d > 0)
        def _():
            pl.semaphore_signal(barrier, inc=1, device_id=(j, lane), device_id_type=MESH)

        @pl.when(lane > 0)
        def _():
            pl.semaphore_signal(barrier, inc=1, device_id=(j, lane - 1), device_id_type=MESH)

        @pl.when(lane < lanes - 1)
        def _():
            pl.semaphore_signal(barrier, inc=1, device_id=(j, lane + 1), device_id_type=MESH)

        return carry

    img_load = pltpu.make_async_copy(img, image.at[:, pl.ds(8, height), :], load.at[0])
    img_load.start()
    lax.fori_loop(0, stacks, greet, 0)

    def greet_lane(d, carry):
        t = lax.rem(lane + d, lanes)

        @pl.when(jnp.logical_or(t > lane + 1, t < lane - 1))
        def _():
            pl.semaphore_signal(barrier, inc=1, device_id=(here, t), device_id_type=MESH)

        return carry

    lax.fori_loop(1, lanes, greet_lane, 0)
    loads = [
        pltpu.make_async_copy(source, target, load.at[i + 1])
        for i, (source, target) in enumerate(
            ((ids, whole_ids), (wide_in, wide), (tall_in, tall), (deep_in, deep), (owner_in, owner))
        )
    ]
    for part in loads:
        part.start()

    @pl.when(lane == 0)
    def _():
        halo[0] = jnp.zeros(halo.shape[1:], F32)

    @pl.when(lane == lanes - 1)
    def _():
        halo[1] = jnp.zeros(halo.shape[1:], F32)

    blank = encode(jnp.zeros((thick, 8, cols), F32))
    image[:, :8, :] = blank
    image[:, 8 + height :, :] = blank
    turned[:, :8, :] = jnp.zeros((2, 8, LANE), F32)
    turned[:, 8 + height :, :] = jnp.zeros((2, 8, LANE), F32)
    square[...] = jnp.zeros(square.shape, F32)
    img_load.wait()
    spot = lax.broadcasted_iota(jnp.int32, (LANE, LANE), 1)
    for y in range(0, height, LANE):
        mixed = jnp.zeros((LANE, LANE), F32)
        for z in range(thick):
            first = image[z, 8 + y : 8 + y + LANE, :LANE]
            last = image[z, 8 + y : 8 + y + LANE, cols - LANE :]
            at = z * HALF
            mixed = jnp.where((spot >= at) & (spot < at + HALF), pltpu.roll(last, (at + HALF) % LANE, 1), mixed)
            at = wide_rows + z * HALF
            mixed = jnp.where((spot >= at) & (spot < at + HALF), pltpu.roll(first, at, 1), mixed)
        both = jnp.transpose(mixed)
        edges[0, :, y : y + LANE] = both[:wide_rows]
        edges[1, :, y : y + LANE] = both[wide_rows : 2 * wide_rows]

    def code(i, carry):
        at = pl.ds(pl.multiple_of(8 + i * 32, 8), 32)
        for z in range(thick):
            image[z, at, :] = encode(image[z, at, :])
        return carry

    lax.fori_loop(0, height // 32, code, 0)

    def main_copy(j, source):
        return pltpu.make_async_remote_copy(
            src_ref=blocks.at[j],
            dst_ref=came.at[source],
            send_sem=send.at[j],
            recv_sem=recv.at[source],
            device_id=(j, lane),
            device_id_type=MESH,
        )

    def side_copy(side, j, source, target):
        return pltpu.make_async_remote_copy(
            src_ref=edges.at[side],
            dst_ref=halo.at[side, source],
            send_sem=side_send.at[side, j],
            recv_sem=side_recv.at[side, source],
            device_id=(j, target),
            device_id_type=MESH,
        )

    sides = lax.div(lane + lanes - 1, lanes) + lax.div(2 * lanes - 2 - lane, lanes)
    pl.semaphore_wait(barrier, stacks - 1 + stacks * sides + lanes - 1 - sides)

    def build(j):
        for z in range(thick):
            view = image.at[z, pl.ds(pl.multiple_of(j * rows, 8), rows + 16), :]
            pack[z * padded : (z + 1) * padded, :] = view[8 - HALF : 8 - HALF + padded, :]
        blocks[j] = pack[...].astype(BF16)

    def side_start(j):
        @pl.when(lane < lanes - 1)
        def _():
            side_copy(0, j, here, lane + 1).start()

        @pl.when(lane > 0)
        def _():
            side_copy(1, j, here, lane - 1).start()

    half = stacks // 2
    upper = (2 * here) // stacks
    rank = here - upper * half

    def near(d):
        pair = lax.rem(rank // 2 + d // 2, half // 2)
        return upper * half + 2 * pair + lax.rem(rank + d, 2)

    def far(d):
        return (1 - upper) * half + lax.rem(rank + d, half)

    def sides_near(d, carry):
        side_start(near(d))
        return carry

    lax.fori_loop(0, half, sides_near, 0)

    def start_near(d, carry):
        build(near(d))
        main_copy(near(d), here).start()
        return carry

    lax.fori_loop(1, half, start_near, 0)
    build(here)
    came[here] = blocks[here]

    def build_far(d, carry):
        build(far(d))
        return carry

    lax.fori_loop(0, half, build_far, 0)

    for e in range(HALF):
        planar[e] = jnp.zeros(planar.shape[1:], F32)
        planar[depth + HALF + e] = jnp.zeros(planar.shape[1:], F32)
    acc[...] = jnp.zeros(acc.shape, F32)
    for part in loads:
        part.wait()

    for kind, part in enumerate((wide, tall, deep)):
        square[kind * 8 : kind * 8 + TAPS, :chans] = part[...]
    flipped = jnp.transpose(square[...])
    tap = [
        jnp.broadcast_to(flipped[:chans, k * 8 + i : k * 8 + i + 1], (chans, LANE))
        for k in range(3)
        for i in range(TAPS)
    ]
    group = TAPS * PART
    half_rows = PART // 2
    for t in range(2):
        line = lax.broadcasted_iota(jnp.int32, (chans, LANE), 1) + t * LANE
        shift_of = line % group // PART
        row_of = line % PART
        kind_of = line // group
        across = jnp.zeros((chans, LANE), F32)
        for b in range(TAPS):
            across = jnp.where((shift_of == b) & (kind_of < 3), tap[b], across)
        for odd in range(2):
            for y in range(half_rows):
                down = jnp.zeros((chans, LANE), F32)
                for a in range(TAPS):
                    down = jnp.where(row_of == y + a + 4 * odd, tap[TAPS + a], down)
                both = across * down
                high = both.astype(BF16)
                low = (both - high.astype(F32)).astype(BF16)
                filt[odd, y * chans : (y + 1) * chans, t * LANE : (t + 1) * LANE] = jnp.where(
                    kind_of == 1, low.astype(F32), high.astype(F32)
                ).astype(BF16)

    strip_spot = lax.broadcasted_iota(jnp.int32, (24, LANE), 1)
    spots = lax.broadcasted_iota(jnp.int32, (size, LANE), 1)

    def shifted(tiles, shift):
        if shift == 0:
            return jnp.concatenate(tiles[1:], axis=1)
        moved = [pltpu.roll(t, (-shift) % LANE, 1) for t in tiles]
        if shift < 0:
            out = [jnp.where(spots < -shift, moved[t - 1], moved[t]) for t in range(1, len(tiles))]
        else:
            out = [
                jnp.where(spots >= LANE - shift, moved[(t + 1) % len(tiles)], moved[t])
                for t in range(1, len(tiles))
            ]
        return jnp.concatenate(out, axis=1)

    def plane(slab, turned, strips):
        for y in range(0, height, LANE):
            turned[8 + y : 8 + y + LANE, :] = jnp.transpose(
                jnp.concatenate(
                    [halo[0, slab, :, y : y + LANE], halo[1, slab, :, y : y + LANE],
                     jnp.zeros((LANE - 2 * wide_rows, LANE), F32)],
                    axis=0,
                )
            )
        strip = turned[pl.ds(here * rows + 8 - HALF, 24), :]
        for z in range(thick):
            left = pltpu.roll(strip, (LANE - HALF - z * HALF) % LANE, 1)
            right = pltpu.roll(strip, (LANE - wide_rows - z * HALF) % LANE, 1)
            strips[z * padded : z * padded + padded, :] = jnp.where(
                strip_spot < LANE // 2, right, left
            )[:padded]
        now = decode(came[slab].astype(F32))
        tiles = [strips[...]] + [now[:, x : x + LANE] for x in range(0, cols, LANE)]
        moved = [shifted(tiles, b - HALF) for b in range(TAPS)]
        high = [t.astype(BF16).astype(F32) for t in moved]
        low = [t - h for t, h in zip(moved, high)]
        rest = jnp.zeros((2 * LANE - 3 * group, cols), BF16)
        for z in range(thick):
            first = z * padded // 8 * 8
            odd = z * padded % 8 // 4
            for y in range(0, rows, half_rows):
                at = slice(first + y, first + y + PART)
                upper = jnp.concatenate([t[at] for t in high], axis=0).astype(BF16)
                lower = jnp.concatenate([t[at] for t in low], axis=0).astype(BF16)
                total = jnp.dot(
                    filt[odd], jnp.concatenate([upper, upper, lower, rest], axis=0),
                    preferred_element_type=F32,
                )
                planar[slab * thick + z + HALF, y * chans : (y + half_rows) * chans, :] = (
                    total.astype(BF16).astype(F32)
                )

    shift = LO.bit_length() - 1
    few = FEW.bit_length() - 1
    many = LO // FEW * highs
    code_line = lax.broadcasted_iota(jnp.int32, (max(many, FEW), LANE), 0).astype(F32).astype(BF16)
    unit = jnp.ones((max(many, FEW), LANE), BF16)
    nil = jnp.zeros((max(many, FEW), LANE), BF16)

    def wider(row, length):
        row = jnp.broadcast_to(row, (16, LANE)).astype(BF16)
        return jnp.concatenate([row] * (length // 16), axis=0)

    def sort(slab, carry):
        for k in range(2 * thick):
            z = slab * 2 * thick + k
            for x in range(0, cols, LANE):
                part = whole_ids[z, :, x : x + LANE]
                high = part >> shift
                low = part & (LO - 1)
                highs_f[x // LANE, z] = high.astype(F32)
                lows_f[x // LANE, z] = low.astype(F32)
                thirds_f[x // LANE, z] = ((low >> few) * highs + high).astype(F32)
                fourths_f[x // LANE, z] = (low & (FEW - 1)).astype(F32)
        for k in range(2 * thick):
            z = slab * 2 * thick + k
            left, right = [], []
            for y in range(rows):
                for x in range(0, cols, LANE):
                    row = wider(thirds_f[x // LANE, z, pl.ds(y, 1), :], many)
                    left.append(jnp.where(row == code_line[:many], unit[:many], nil[:many]))
                    row = wider(fourths_f[x // LANE, z, pl.ds(y, 1), :], FEW)
                    right.append(jnp.where(row == code_line[:FEW], unit[:FEW], nil[:FEW]))
            counts[...] += lax.dot_general(
                jnp.concatenate(left, axis=1), jnp.concatenate(right, axis=1),
                (((1,), (1,)), ((), ())), preferred_element_type=F32,
            )
        return carry

    counts[...] = jnp.zeros(counts.shape, F32)
    def send_far(d, carry):
        main_copy(far(d), here).start()
        side_start(far(d))
        return carry

    inner = jnp.where(upper == 0, rank, half - 1 - rank) * 2 >= half

    @pl.when(inner)
    def _():
        lax.fori_loop(0, half, send_far, 0)

    lax.fori_loop(0, half // 2, sort, 0)
    taken = jnp.concatenate([(owner[...] == t).astype(F32) for t in range(lanes)], axis=0)
    lines = lanes * highs
    over = lax.broadcasted_iota(jnp.int32, (LANE, LANE), 0)
    under = lax.broadcasted_iota(jnp.int32, (LANE, LANE), 1)
    within = jnp.dot(
        taken.astype(BF16), (over < under).astype(F32).astype(BF16), preferred_element_type=F32
    )
    summed = jnp.dot(taken.astype(BF16), jnp.ones((LANE, LANE), BF16), preferred_element_type=F32)
    over = lax.broadcasted_iota(jnp.int32, (lines, lines), 0)
    under = lax.broadcasted_iota(jnp.int32, (lines, lines), 1)
    before = jnp.logical_and(over // highs == under // highs, under < over).astype(F32).astype(BF16)
    within = within + jnp.dot(before, summed.astype(BF16), preferred_element_type=F32)
    slots[...] = jnp.where(taken > 0.5, within, -1.0)

    def start_far(d, carry):
        @pl.when(d > 0)
        def _():
            main_copy(near(d), here).wait_send()

        return carry

    @pl.when(jnp.logical_not(inner))
    def _():
        lax.fori_loop(0, half, start_far, 0)
        lax.fori_loop(0, half, send_far, 0)

    lax.fori_loop(half // 2, half, sort, 0)

    @pl.when(inner)
    def _():
        lax.fori_loop(0, half, start_far, 0)


    low_line = lax.broadcasted_iota(jnp.int32, (LO, LANE), 0).astype(F32).astype(BF16)
    high_line = (lax.broadcasted_iota(jnp.int32, (highs * chans, LANE), 0) // chans).astype(F32).astype(BF16)
    one = jnp.ones((LO, LANE), BF16)
    zero = jnp.zeros((LO, LANE), BF16)
    none = jnp.zeros((highs * chans, LANE), BF16)

    def count(z):
        left, right = [], []
        for y in range(rows):
            for x in range(0, cols, LANE):
                at = slice(y * chans, (y + 1) * chans)
                total = tap[2 * TAPS] * planar[z, at, x : x + LANE]
                for e in range(1, TAPS):
                    total = total + tap[2 * TAPS + e] * planar[z + e, at, x : x + LANE]
                feat = jnp.tanh(total).astype(BF16)
                high = highs_f[x // LANE, z, pl.ds(y, 1), :]
                low = lows_f[x // LANE, z, pl.ds(y, 1), :]
                left.append(jnp.where(
                    wider(high, highs * chans) == high_line,
                    jnp.concatenate([feat] * highs, axis=0), none,
                ))
                right.append(jnp.where(wider(low, LO) == low_line, one, zero))
        return left, right

    def tally(which):
        for k in range(0, thick, 2):
            left, right = [], []
            for more in range(2):
                parts = count(lax.rem(which * thick + HALF + k + more, depth))
                left += parts[0]
                right += parts[1]
            acc[...] += lax.dot_general(
                jnp.concatenate(left, axis=1), jnp.concatenate(right, axis=1),
                (((1,), (1,)), ((), ())), preferred_element_type=F32,
            )

    def arrive(slab):
        @pl.when(slab != here)
        def _():
            main_copy(slab, slab).wait_recv()

        @pl.when(lane < lanes - 1)
        def _():
            side_copy(1, slab, slab, lane + 1).wait_recv()

        @pl.when(lane > 0)
        def _():
            side_copy(0, slab, slab, lane - 1).wait_recv()

    inmost = jnp.where(upper == 0, rank, half - 1 - rank) // 2 * 2

    def mirrored(i, top):
        return upper * top + (1 - 2 * upper) * i

    def place(i):
        i = jnp.where(i <= 1, inmost + i, jnp.where(i <= inmost + 1, inmost + 1 - i, i))
        return mirrored(i, stacks - 1)

    def unit(i):
        turn = mirrored(jnp.where(i <= inmost, inmost - i, i), stacks - 2)
        return jnp.where(i == stacks - 1, stacks - 1, turn)

    arrive(place(0))
    arrive(place(1))
    for i in range(2):
        plane(place(i), turned.at[i], strips.at[i])

    def work(i, carry):
        arrive(place(i + 2))
        tally(unit(i))
        plane(place(i + 2), turned.at[0], strips.at[0])
        return carry

    lax.fori_loop(0, stacks - 2, work, 0)

    def close(i, carry):
        tally(unit(i))
        return carry

    lax.fori_loop(stacks - 2, stacks, close, 0)

    def drain(d, carry):
        main_copy(far(d), here).wait_send()
        return carry

    lax.fori_loop(0, half, drain, 0)

    def finish(d, carry):
        j = lax.rem(here + d, stacks)

        @pl.when(lane < lanes - 1)
        def _():
            side_copy(0, j, here, lane + 1).wait_send()

        @pl.when(lane > 0)
        def _():
            side_copy(1, j, here, lane - 1).wait_send()

        return carry

    lax.fori_loop(0, stacks, finish, 0)
    every = jnp.concatenate(
        [counts[q * highs : (q + 1) * highs, :] for q in range(LO // FEW)], axis=1
    )
    kind = lax.broadcasted_iota(jnp.int32, (chans, LANE), 0)
    left = []
    for h in range(highs):
        count_row = every[h : h + 1, :]
        mean = acc[h * chans : (h + 1) * chans, :] / count_row
        means_ref[:, h * LO : (h + 1) * LO] = mean
        tally_parts = [jnp.broadcast_to(p.astype(F32), (chans, LANE)) for p in split3(count_row)]
        rows_of = jnp.where(kind == 0, tally_parts[0], jnp.where(kind == 1, tally_parts[1], tally_parts[2]))
        rows_of = jnp.where(kind < 3, rows_of, 0.0).astype(BF16)
        left.append(jnp.concatenate(list(split3(mean)) + [rows_of], axis=0))
    means_out.start()
    left = jnp.concatenate(left, axis=1)
    cap = pay.shape[2]
    slot_line = lax.broadcasted_iota(jnp.int32, (cap // 2, LANE), 0).astype(F32).astype(BF16)
    full = jnp.ones((cap // 2, LANE), BF16)
    bare = jnp.zeros((cap // 2, LANE), BF16)

    def pay_copy(target, source):
        return pltpu.make_async_remote_copy(
            src_ref=pay.at[target],
            dst_ref=gathered.at[source],
            send_sem=pay_send.at[target],
            recv_sem=pay_recv.at[source],
            device_id=(here, target),
            device_id_type=MESH,
        )

    def share(d, carry):
        t = lax.rem(lane + d, lanes)
        right = []
        for h in range(highs):
            row = slots[pl.ds(t * highs + h, 1), :]
            right.append(jnp.concatenate(
                [jnp.where(wider(row - float(p), cap // 2) == slot_line, full, bare)
                 for p in (0, cap // 2)],
                axis=0,
            ))
        out = lax.dot_general(
            left, jnp.concatenate(right, axis=1), (((1,), (1,)), ((), ())),
            preferred_element_type=F32,
        )
        pay[t, :chans, :] = out[:chans] + out[chans : 2 * chans] + out[2 * chans : 3 * chans]
        weight = out[3 * chans : 3 * chans + 1] + out[3 * chans + 1 : 3 * chans + 2] + out[3 * chans + 2 : 3 * chans + 3]
        pay[t, chans:, :] = jnp.broadcast_to(weight, (pay.shape[1] - chans, cap))

        @pl.when(d < lanes)
        def _():
            pay_copy(t, lane).start()

        return carry

    lax.fori_loop(1, lanes + 1, share, 0)
    own_pay = pltpu.make_async_copy(pay.at[lane], gathered.at[lane], load.at[0])
    own_pay.start()
    def settle(d, carry):
        t = lax.rem(lane + d, lanes)
        pay_copy(t, lane).wait_send()
        pay_copy(t, t).wait_recv()
        return carry

    lax.fori_loop(1, lanes, settle, 0)
    own_pay.wait()
    means_out.wait()


def split3(x):
    high = x.astype(BF16)
    rest = x - high.astype(F32)
    mid = rest.astype(BF16)
    low = (rest - mid.astype(F32)).astype(BF16)
    return high, mid, low


def refine_kernel(
    pseudo, pay_in, means, coarse_in, parent_in, offsets_in, means_ref, out_ref,
    pay, coarse, parent, offsets, factors, norms, load,
):
    loads = [
        pltpu.make_async_copy(source, target, load.at[i])
        for i, (source, target) in enumerate(
            ((pay_in, pay), (coarse_in, coarse), (parent_in, parent), (offsets_in, offsets), (means, means_ref))
        )
    ]
    for part in loads:
        part.start()
    for part in loads[:-1]:
        part.wait()
    sources, _, fragments = pay.shape
    chans = out_ref.shape[0]
    coarse_count = coarse.shape[1]
    fine = out_ref.shape[1]
    select = (
        jnp.broadcast_to(parent[...], (coarse_count, fine))
        == lax.broadcasted_iota(jnp.int32, (coarse_count, fine), 0)
    ).astype(F32)
    cents = jnp.dot(coarse[...], select, precision=HIGH, preferred_element_type=F32) + offsets[...]

    def prepare(s, carry):
        frags = pay[s, :chans, :]
        fh, fm, fl = split3(2.0 * sharpness * frags)
        ones = jnp.full((3 * chans, fragments), -sharpness, BF16)
        factors[s] = jnp.concatenate([fh, fm, fh, fl, fm, fh, ones], axis=0)
        norms[s] = -sharpness * jnp.sum(frags * frags, axis=0, keepdims=True)
        return carry

    lax.fori_loop(0, sources, prepare, 0)

    def iterate(step, cents):
        ch, cm, cl = split3(cents)
        sh, sm, sl = split3(cents * cents)
        keys = jnp.concatenate([ch, ch, cm, ch, cm, cl, sh, sm, sl], axis=0)

        def visit(s, total):
            scores = norms[s] + lax.dot_general(
                keys, factors[s], (((0,), (0,)), ((), ())), preferred_element_type=F32
            )
            top = jnp.max(scores, axis=0, keepdims=True)
            expo = jnp.exp(scores - top)
            scale = pay[s, chans : chans + 1, :] / jnp.sum(expo, axis=0, keepdims=True)
            scale = jnp.broadcast_to(scale, (chans, fragments))
            gh, gm, gl = split3(jnp.concatenate([pay[s, :chans, :] * scale, scale], axis=0))
            eh = expo.astype(BF16)
            em = (expo - eh.astype(F32)).astype(BF16)
            dims = (((1,), (1,)), ((), ()))
            first = lax.dot_general(
                jnp.concatenate([gh, gm, gl], axis=0), eh, dims, preferred_element_type=F32
            )
            second = lax.dot_general(
                jnp.concatenate([gh, gm], axis=0), em, dims, preferred_element_type=F32
            )
            size = 2 * chans
            return (
                total
                + (first[2 * size :] + second[size:])
                + (first[size : 2 * size] + second[:size])
                + first[:size]
            )

        total = lax.fori_loop(
            0, sources, visit, jnp.zeros((2 * chans, fine), F32), unroll=4
        )
        return (total[:chans] + pseudo * cents) / (total[chans:] + pseudo)

    out_ref[...] = lax.fori_loop(0, ITERS, iterate, cents)
    loads[-1].wait()


def shards(
    slab_image,
    width_taps,
    height_taps,
    depth_taps,
    fragment_ids,
    fragment_owner,
    coarse_centroids,
    parent_map,
    fine_offsets,
):
    chans = width_taps.shape[0]
    depth, rows, cols = fragment_ids.shape
    fragments = fragment_owner.shape[0]
    lanes = lax.axis_size("xy")
    stacks = lax.axis_size("gz")
    padded_rows = rows + TAPS - 1
    slab_depth, height, _ = slab_image.shape
    highs = fragments // LO
    assert highs <= 16
    cap = min(CAP, fragments)
    gathered, means = pl.pallas_call(
        pencil_kernel,
        out_shape=(
            jax.ShapeDtypeStruct((lanes, chans + 8, cap), F32),
            jax.ShapeDtypeStruct((chans, fragments), F32),
        ),
        in_specs=[pl.BlockSpec(memory_space=pltpu.HBM)] * 6,
        out_specs=(pl.BlockSpec(memory_space=pltpu.HBM),) * 2,
        scratch_shapes=[
            pltpu.VMEM((slab_depth, height + 16, cols), F32),
            pltpu.VMEM((stacks, slab_depth * padded_rows, cols), BF16),
            pltpu.VMEM((stacks, slab_depth * padded_rows, cols), BF16),
            pltpu.VMEM((slab_depth * padded_rows, cols), F32),
            pltpu.VMEM((2, slab_depth * padded_rows, LANE), F32),
            pltpu.VMEM((2, slab_depth * HALF, height), F32),
            pltpu.VMEM((2, stacks, slab_depth * HALF, height), F32),
            pltpu.VMEM((2, height + 16, LANE), F32),
            pltpu.VMEM((LANE, LANE), F32),
            pltpu.VMEM((2, LANE, 2 * LANE), BF16),
            pltpu.VMEM((depth + 2 * HALF, rows * chans, cols), F32),
            pltpu.VMEM((depth, rows, cols), jnp.int32),
            pltpu.VMEM((cols // LANE, depth, rows, LANE), F32),
            pltpu.VMEM((cols // LANE, depth, rows, LANE), F32),
            pltpu.VMEM((cols // LANE, depth, rows, LANE), F32),
            pltpu.VMEM((cols // LANE, depth, rows, LANE), F32),
            pltpu.VMEM((highs * chans, LO), F32),
            pltpu.VMEM((LO // FEW * highs, FEW), F32),
            pltpu.VMEM((TAPS, chans), F32),
            pltpu.VMEM((TAPS, chans), F32),
            pltpu.VMEM((TAPS, chans), F32),
            pltpu.VMEM((highs, LANE), jnp.int32),
            pltpu.VMEM((lanes * highs, LANE), F32),
            pltpu.VMEM((lanes, chans + 8, cap), F32),
            pltpu.VMEM((chans, fragments), F32),
            pltpu.SemaphoreType.DMA((6,)),
            pltpu.SemaphoreType.DMA((stacks,)),
            pltpu.SemaphoreType.DMA((stacks,)),
            pltpu.SemaphoreType.DMA((2, stacks)),
            pltpu.SemaphoreType.DMA((2, stacks)),
            pltpu.SemaphoreType.DMA((lanes,)),
            pltpu.SemaphoreType.DMA((lanes,)),
        ],
        compiler_params=pltpu.CompilerParams(
            collective_id=0, has_side_effects=True, vmem_limit_bytes=60 << 20
        ),
        name="pencil",
    )(slab_image, fragment_ids, width_taps.T, height_taps.T, depth_taps.T, fragment_owner.reshape(highs, LANE))
    fine = fine_offsets.shape[1]
    pseudo = float(fragment_ids.size // fine)
    return pl.pallas_call(
        functools.partial(refine_kernel, pseudo),
        out_shape=(
            jax.ShapeDtypeStruct((chans, fragments), F32),
            jax.ShapeDtypeStruct((chans, fine), F32),
        ),
        in_specs=[pl.BlockSpec(memory_space=pltpu.HBM)] * 5,
        out_specs=(pl.BlockSpec(memory_space=pltpu.HBM), pl.BlockSpec(memory_space=pltpu.VMEM)),
        scratch_shapes=[
            pltpu.VMEM((lanes, chans + 8, cap), F32),
            pltpu.VMEM(coarse_centroids.shape, F32),
            pltpu.VMEM((1, fine), jnp.int32),
            pltpu.VMEM((chans, fine), F32),
            pltpu.VMEM((lanes, 9 * chans, cap), BF16),
            pltpu.VMEM((lanes, 1, cap), F32),
            pltpu.SemaphoreType.DMA((5,)),
        ],
        compiler_params=pltpu.CompilerParams(vmem_limit_bytes=60 << 20),
        name="refine",
    )(gathered, means, coarse_centroids, parent_map.reshape(1, fine), fine_offsets)


def solution(mesh):
    placed = (
        P("gz", None, "xy"),
        P(),
        P(),
        P(),
        P(None, "gz", "xy"),
        P(("gz", "xy"), None),
        P(None, ("gz", "xy")),
        P(("gz", "xy")),
        P(None, ("gz", "xy")),
    )
    return jax.shard_map(
        shards,
        mesh=mesh,
        in_specs=placed,
        out_specs=(P(None, ("gz", "xy")), P(None, ("gz", "xy"))),
        check_vma=False,
    )
```

```python
import functools

import jax
import jax.numpy as jnp
from jax import lax
from jax.experimental import pallas as pl
from jax.experimental.pallas import tpu as pltpu
from jax.sharding import PartitionSpec as P

TAPS = 5
HALF = TAPS // 2
ITERS = 3
HIGH = lax.Precision.HIGHEST
sharpness = 2.0
LO = 128
F32 = jnp.float32
BF16 = jnp.bfloat16


MESH = pl.DeviceIdType.MESH
LANE = 128
PART = 16
FEW = 32
CAP = 512
SPREAD = 240.0


def encode(x):
    return jnp.exp2((x - 0.5) * SPREAD)


def decode(x):
    return jnp.log2(x) * (1.0 / SPREAD) + 0.5


def pencil_kernel(
    img, ids, wide_in, tall_in, deep_in, owner_in, gathered, means_to,
    image, blocks, came, pack, strips, edges, halo, turned, square, filt,
    planar, whole_ids, highs_f, lows_f, thirds_f, fourths_f, acc, counts, wide, tall, deep, owner, slots, pay, means_ref,
    load, send, recv, side_send, side_recv, pay_send, pay_recv,
):
    here = lax.axis_index("gz")
    lane = lax.axis_index("xy")
    stacks = lax.axis_size("gz")
    lanes = lax.axis_size("xy")
    thick, height, cols = img.shape
    depth, rows, _ = ids.shape
    padded = rows + TAPS - 1
    size = thick * padded
    wide_rows = thick * HALF
    chans, fragments = means_ref.shape
    highs = fragments // LO
    means_out = pltpu.make_async_copy(means_ref, means_to, load.at[1])

    barrier = pltpu.get_barrier_semaphore()

    def greet(d, carry):
        j = lax.rem(here + d, stacks)

        @pl.when(d > 0)
        def _():
            pl.semaphore_signal(barrier, inc=1, device_id=(j, lane), device_id_type=MESH)

        @pl.when(lane > 0)
        def _():
            pl.semaphore_signal(barrier, inc=1, device_id=(j, lane - 1), device_id_type=MESH)

        @pl.when(lane < lanes - 1)
        def _():
            pl.semaphore_signal(barrier, inc=1, device_id=(j, lane + 1), device_id_type=MESH)

        return carry

    img_load = pltpu.make_async_copy(img, image.at[:, pl.ds(8, height), :], load.at[0])
    img_load.start()
    lax.fori_loop(0, stacks, greet, 0)

    def greet_lane(d, carry):
        t = lax.rem(lane + d, lanes)

        @pl.when(jnp.logical_or(t > lane + 1, t < lane - 1))
        def _():
            pl.semaphore_signal(barrier, inc=1, device_id=(here, t), device_id_type=MESH)

        return carry

    lax.fori_loop(1, lanes, greet_lane, 0)
    loads = [
        pltpu.make_async_copy(source, target, load.at[i + 1])
        for i, (source, target) in enumerate(
            ((ids, whole_ids), (wide_in, wide), (tall_in, tall), (deep_in, deep), (owner_in, owner))
        )
    ]
    for part in loads:
        part.start()

    @pl.when(lane == 0)
    def _():
        halo[0] = jnp.zeros(halo.shape[1:], F32)

    @pl.when(lane == lanes - 1)
    def _():
        halo[1] = jnp.zeros(halo.shape[1:], F32)

    blank = encode(jnp.zeros((thick, 8, cols), F32))
    image[:, :8, :] = blank
    image[:, 8 + height :, :] = blank
    turned[:8, :] = jnp.zeros((8, LANE), F32)
    turned[8 + height :, :] = jnp.zeros((8, LANE), F32)
    square[...] = jnp.zeros(square.shape, F32)
    img_load.wait()
    spot = lax.broadcasted_iota(jnp.int32, (LANE, LANE), 1)
    for y in range(0, height, LANE):
        mixed = jnp.zeros((LANE, LANE), F32)
        for z in range(thick):
            first = image[z, 8 + y : 8 + y + LANE, :LANE]
            last = image[z, 8 + y : 8 + y + LANE, cols - LANE :]
            at = z * HALF
            mixed = jnp.where((spot >= at) & (spot < at + HALF), pltpu.roll(last, (at + HALF) % LANE, 1), mixed)
            at = wide_rows + z * HALF
            mixed = jnp.where((spot >= at) & (spot < at + HALF), pltpu.roll(first, at, 1), mixed)
        both = jnp.transpose(mixed)
        edges[0, :, y : y + LANE] = both[:wide_rows]
        edges[1, :, y : y + LANE] = both[wide_rows : 2 * wide_rows]

    def code(i, carry):
        at = pl.ds(pl.multiple_of(8 + i * 32, 8), 32)
        for z in range(thick):
            image[z, at, :] = encode(image[z, at, :])
        return carry

    lax.fori_loop(0, height // 32, code, 0)

    def main_copy(j, source):
        return pltpu.make_async_remote_copy(
            src_ref=blocks.at[j],
            dst_ref=came.at[source],
            send_sem=send.at[j],
            recv_sem=recv.at[source],
            device_id=(j, lane),
            device_id_type=MESH,
        )

    def side_copy(side, j, source, target):
        return pltpu.make_async_remote_copy(
            src_ref=edges.at[side],
            dst_ref=halo.at[side, source],
            send_sem=side_send.at[side, j],
            recv_sem=side_recv.at[side, source],
            device_id=(j, target),
            device_id_type=MESH,
        )

    sides = lax.div(lane + lanes - 1, lanes) + lax.div(2 * lanes - 2 - lane, lanes)
    pl.semaphore_wait(barrier, stacks - 1 + stacks * sides + lanes - 1 - sides)

    def build(j):
        for z in range(thick):
            view = image.at[z, pl.ds(pl.multiple_of(j * rows, 8), rows + 16), :]
            pack[z * padded : (z + 1) * padded, :] = view[8 - HALF : 8 - HALF + padded, :]
        blocks[j] = pack[...].astype(BF16)

    def side_start(j):
        @pl.when(lane < lanes - 1)
        def _():
            side_copy(0, j, here, lane + 1).start()

        @pl.when(lane > 0)
        def _():
            side_copy(1, j, here, lane - 1).start()

    half = stacks // 2
    upper = (2 * here) // stacks
    rank = here - upper * half

    def near(d):
        pair = lax.rem(rank // 2 + d // 2, half // 2)
        return upper * half + 2 * pair + lax.rem(rank + d, 2)

    def far(d):
        return (1 - upper) * half + lax.rem(rank + d, half)

    def start_near(d, carry):
        j = near(d)
        build(j)

        @pl.when(d > 0)
        def _():
            main_copy(j, here).start()

        side_start(j)
        return carry

    lax.fori_loop(0, half, start_near, 0)
    came[here] = blocks[here]

    def build_far(d, carry):
        build(far(d))
        return carry

    lax.fori_loop(0, half, build_far, 0)

    for e in range(HALF):
        planar[e] = jnp.zeros(planar.shape[1:], F32)
        planar[depth + HALF + e] = jnp.zeros(planar.shape[1:], F32)
    acc[...] = jnp.zeros(acc.shape, F32)
    for part in loads:
        part.wait()

    for kind, part in enumerate((wide, tall, deep)):
        square[kind * 8 : kind * 8 + TAPS, :chans] = part[...]
    flipped = jnp.transpose(square[...])
    tap = [
        jnp.broadcast_to(flipped[:chans, k * 8 + i : k * 8 + i + 1], (chans, LANE))
        for k in range(3)
        for i in range(TAPS)
    ]
    group = TAPS * PART
    half_rows = PART // 2
    for t in range(2):
        line = lax.broadcasted_iota(jnp.int32, (chans, LANE), 1) + t * LANE
        shift_of = line % group // PART
        row_of = line % PART
        kind_of = line // group
        across = jnp.zeros((chans, LANE), F32)
        for b in range(TAPS):
            across = jnp.where((shift_of == b) & (kind_of < 3), tap[b], across)
        for odd in range(2):
            for y in range(half_rows):
                down = jnp.zeros((chans, LANE), F32)
                for a in range(TAPS):
                    down = jnp.where(row_of == y + a + 4 * odd, tap[TAPS + a], down)
                both = across * down
                high = both.astype(BF16)
                low = (both - high.astype(F32)).astype(BF16)
                filt[odd, y * chans : (y + 1) * chans, t * LANE : (t + 1) * LANE] = jnp.where(
                    kind_of == 1, low.astype(F32), high.astype(F32)
                ).astype(BF16)

    strip_spot = lax.broadcasted_iota(jnp.int32, (24, LANE), 1)
    spots = lax.broadcasted_iota(jnp.int32, (size, LANE), 1)

    def shifted(tiles, shift):
        if shift == 0:
            return jnp.concatenate(tiles[1:], axis=1)
        moved = [pltpu.roll(t, (-shift) % LANE, 1) for t in tiles]
        if shift < 0:
            out = [jnp.where(spots < -shift, moved[t - 1], moved[t]) for t in range(1, len(tiles))]
        else:
            out = [
                jnp.where(spots >= LANE - shift, moved[(t + 1) % len(tiles)], moved[t])
                for t in range(1, len(tiles))
            ]
        return jnp.concatenate(out, axis=1)

    def plane(slab):
        for y in range(0, height, LANE):
            turned[8 + y : 8 + y + LANE, :] = jnp.transpose(
                jnp.concatenate(
                    [halo[0, slab, :, y : y + LANE], halo[1, slab, :, y : y + LANE],
                     jnp.zeros((LANE - 2 * wide_rows, LANE), F32)],
                    axis=0,
                )
            )
        strip = turned[pl.ds(here * rows + 8 - HALF, 24), :]
        for z in range(thick):
            left = pltpu.roll(strip, (LANE - HALF - z * HALF) % LANE, 1)
            right = pltpu.roll(strip, (LANE - wide_rows - z * HALF) % LANE, 1)
            strips[z * padded : z * padded + padded, :] = jnp.where(
                strip_spot < LANE // 2, right, left
            )[:padded]
        now = decode(came[slab].astype(F32))
        tiles = [strips[...]] + [now[:, x : x + LANE] for x in range(0, cols, LANE)]
        moved = [shifted(tiles, b - HALF) for b in range(TAPS)]
        high = [t.astype(BF16).astype(F32) for t in moved]
        low = [t - h for t, h in zip(moved, high)]
        rest = jnp.zeros((2 * LANE - 3 * group, cols), BF16)
        for z in range(thick):
            first = z * padded // 8 * 8
            odd = z * padded % 8 // 4
            for y in range(0, rows, half_rows):
                at = slice(first + y, first + y + PART)
                upper = jnp.concatenate([t[at] for t in high], axis=0).astype(BF16)
                lower = jnp.concatenate([t[at] for t in low], axis=0).astype(BF16)
                total = jnp.dot(
                    filt[odd], jnp.concatenate([upper, upper, lower, rest], axis=0),
                    preferred_element_type=F32,
                )
                planar[slab * thick + z + HALF, y * chans : (y + half_rows) * chans, :] = (
                    total.astype(BF16).astype(F32)
                )

    shift = LO.bit_length() - 1
    few = FEW.bit_length() - 1
    many = LO // FEW * highs
    code_line = lax.broadcasted_iota(jnp.int32, (max(many, FEW), LANE), 0).astype(F32).astype(BF16)
    unit = jnp.ones((max(many, FEW), LANE), BF16)
    nil = jnp.zeros((max(many, FEW), LANE), BF16)

    def wider(row, length):
        row = jnp.broadcast_to(row, (16, LANE)).astype(BF16)
        return jnp.concatenate([row] * (length // 16), axis=0)

    def sort(slab, carry):
        left, right = [], []
        for k in range(2 * thick):
            z = slab * 2 * thick + k
            for x in range(0, cols, LANE):
                part = whole_ids[z, :, x : x + LANE]
                high = part >> shift
                low = part & (LO - 1)
                highs_f[x // LANE, z] = high.astype(F32)
                lows_f[x // LANE, z] = low.astype(F32)
                thirds_f[x // LANE, z] = ((low >> few) * highs + high).astype(F32)
                fourths_f[x // LANE, z] = (low & (FEW - 1)).astype(F32)
        for k in range(2 * thick):
            z = slab * 2 * thick + k
            for y in range(rows):
                for x in range(0, cols, LANE):
                    row = wider(thirds_f[x // LANE, z, pl.ds(y, 1), :], many)
                    left.append(jnp.where(row == code_line[:many], unit[:many], nil[:many]))
                    row = wider(fourths_f[x // LANE, z, pl.ds(y, 1), :], FEW)
                    right.append(jnp.where(row == code_line[:FEW], unit[:FEW], nil[:FEW]))
        counts[...] += lax.dot_general(
            jnp.concatenate(left, axis=1), jnp.concatenate(right, axis=1),
            (((1,), (1,)), ((), ())), preferred_element_type=F32,
        )
        return carry

    counts[...] = jnp.zeros(counts.shape, F32)
    def send_far(d, carry):
        main_copy(far(d), here).start()
        side_start(far(d))
        return carry

    inner = jnp.where(upper == 0, rank, half - 1 - rank) * 2 >= half

    @pl.when(inner)
    def _():
        lax.fori_loop(0, half, send_far, 0)

    lax.fori_loop(0, half // 2, sort, 0)
    taken = jnp.concatenate([(owner[...] == t).astype(F32) for t in range(lanes)], axis=0)
    lines = lanes * highs
    over = lax.broadcasted_iota(jnp.int32, (LANE, LANE), 0)
    under = lax.broadcasted_iota(jnp.int32, (LANE, LANE), 1)
    within = jnp.dot(
        taken.astype(BF16), (over < under).astype(F32).astype(BF16), preferred_element_type=F32
    )
    summed = jnp.dot(taken.astype(BF16), jnp.ones((LANE, LANE), BF16), preferred_element_type=F32)
    over = lax.broadcasted_iota(jnp.int32, (lines, lines), 0)
    under = lax.broadcasted_iota(jnp.int32, (lines, lines), 1)
    before = jnp.logical_and(over // highs == under // highs, under < over).astype(F32).astype(BF16)
    within = within + jnp.dot(before, summed.astype(BF16), preferred_element_type=F32)
    slots[...] = jnp.where(taken > 0.5, within, -1.0)

    def start_far(d, carry):
        @pl.when(d > 0)
        def _():
            main_copy(near(d), here).wait_send()

        return carry

    @pl.when(jnp.logical_not(inner))
    def _():
        lax.fori_loop(0, half, start_far, 0)
        lax.fori_loop(0, half, send_far, 0)

    lax.fori_loop(half // 2, half, sort, 0)

    @pl.when(inner)
    def _():
        lax.fori_loop(0, half, start_far, 0)


    low_line = lax.broadcasted_iota(jnp.int32, (LO, LANE), 0).astype(F32).astype(BF16)
    high_line = (lax.broadcasted_iota(jnp.int32, (highs * chans, LANE), 0) // chans).astype(F32).astype(BF16)
    one = jnp.ones((LO, LANE), BF16)
    zero = jnp.zeros((LO, LANE), BF16)
    none = jnp.zeros((highs * chans, LANE), BF16)

    def count(z):
        left, right = [], []
        for y in range(rows):
            for x in range(0, cols, LANE):
                at = slice(y * chans, (y + 1) * chans)
                total = tap[2 * TAPS] * planar[z, at, x : x + LANE]
                for e in range(1, TAPS):
                    total = total + tap[2 * TAPS + e] * planar[z + e, at, x : x + LANE]
                feat = jnp.tanh(total).astype(BF16)
                high = highs_f[x // LANE, z, pl.ds(y, 1), :]
                low = lows_f[x // LANE, z, pl.ds(y, 1), :]
                left.append(jnp.where(
                    wider(high, highs * chans) == high_line,
                    jnp.concatenate([feat] * highs, axis=0), none,
                ))
                right.append(jnp.where(wider(low, LO) == low_line, one, zero))
        return left, right

    def tally(which):
        for k in range(0, thick, 2):
            left, right = [], []
            for more in range(2):
                parts = count(lax.rem(which * thick + HALF + k + more, depth))
                left += parts[0]
                right += parts[1]
            acc[...] += lax.dot_general(
                jnp.concatenate(left, axis=1), jnp.concatenate(right, axis=1),
                (((1,), (1,)), ((), ())), preferred_element_type=F32,
            )

    def arrive(slab):
        @pl.when(slab != here)
        def _():
            main_copy(slab, slab).wait_recv()

        @pl.when(lane < lanes - 1)
        def _():
            side_copy(1, slab, slab, lane + 1).wait_recv()

        @pl.when(lane > 0)
        def _():
            side_copy(0, slab, slab, lane - 1).wait_recv()

    inmost = jnp.where(upper == 0, rank, half - 1 - rank) // 2 * 2

    def mirrored(i, top):
        return upper * top + (1 - 2 * upper) * i

    def place(i):
        i = jnp.where(i <= 1, inmost + i, jnp.where(i <= inmost + 1, inmost + 1 - i, i))
        return mirrored(i, stacks - 1)

    def unit(i):
        turn = mirrored(jnp.where(i <= inmost, inmost - i, i), stacks - 2)
        return jnp.where(i == stacks - 1, stacks - 1, turn)

    def prepare(i, carry):
        arrive(place(i))
        plane(place(i))
        return carry

    lax.fori_loop(0, 2, prepare, 0)

    def work(i, carry):
        arrive(place(i + 2))
        tally(unit(i))
        plane(place(i + 2))
        return carry

    lax.fori_loop(0, stacks - 2, work, 0)

    def close(i, carry):
        tally(unit(i))
        return carry

    lax.fori_loop(stacks - 2, stacks, close, 0)

    def drain(d, carry):
        main_copy(far(d), here).wait_send()
        return carry

    lax.fori_loop(0, half, drain, 0)

    def finish(d, carry):
        j = lax.rem(here + d, stacks)

        @pl.when(lane < lanes - 1)
        def _():
            side_copy(0, j, here, lane + 1).wait_send()

        @pl.when(lane > 0)
        def _():
            side_copy(1, j, here, lane - 1).wait_send()

        return carry

    lax.fori_loop(0, stacks, finish, 0)
    every = jnp.concatenate(
        [counts[q * highs : (q + 1) * highs, :] for q in range(LO // FEW)], axis=1
    )
    kind = lax.broadcasted_iota(jnp.int32, (chans, LANE), 0)
    left = []
    for h in range(highs):
        count_row = every[h : h + 1, :]
        mean = acc[h * chans : (h + 1) * chans, :] / count_row
        means_ref[:, h * LO : (h + 1) * LO] = mean
        tally_parts = [jnp.broadcast_to(p.astype(F32), (chans, LANE)) for p in split3(count_row)]
        rows_of = jnp.where(kind == 0, tally_parts[0], jnp.where(kind == 1, tally_parts[1], tally_parts[2]))
        rows_of = jnp.where(kind < 3, rows_of, 0.0).astype(BF16)
        left.append(jnp.concatenate(list(split3(mean)) + [rows_of], axis=0))
    means_out.start()
    left = jnp.concatenate(left, axis=1)
    cap = pay.shape[2]
    slot_line = lax.broadcasted_iota(jnp.int32, (cap // 2, LANE), 0).astype(F32).astype(BF16)
    full = jnp.ones((cap // 2, LANE), BF16)
    bare = jnp.zeros((cap // 2, LANE), BF16)

    def pay_copy(target, source):
        return pltpu.make_async_remote_copy(
            src_ref=pay.at[target],
            dst_ref=gathered.at[source],
            send_sem=pay_send.at[target],
            recv_sem=pay_recv.at[source],
            device_id=(here, target),
            device_id_type=MESH,
        )

    def share(d, carry):
        t = lax.rem(lane + d, lanes)
        right = []
        for h in range(highs):
            row = slots[pl.ds(t * highs + h, 1), :]
            right.append(jnp.concatenate(
                [jnp.where(wider(row - float(p), cap // 2) == slot_line, full, bare)
                 for p in (0, cap // 2)],
                axis=0,
            ))
        out = lax.dot_general(
            left, jnp.concatenate(right, axis=1), (((1,), (1,)), ((), ())),
            preferred_element_type=F32,
        )
        pay[t, :chans, :] = out[:chans] + out[chans : 2 * chans] + out[2 * chans : 3 * chans]
        weight = out[3 * chans : 3 * chans + 1] + out[3 * chans + 1 : 3 * chans + 2] + out[3 * chans + 2 : 3 * chans + 3]
        pay[t, chans:, :] = jnp.broadcast_to(weight, (pay.shape[1] - chans, cap))

        @pl.when(d < lanes)
        def _():
            pay_copy(t, lane).start()

        return carry

    lax.fori_loop(1, lanes + 1, share, 0)
    own_pay = pltpu.make_async_copy(pay.at[lane], gathered.at[lane], load.at[0])
    own_pay.start()
    def settle(d, carry):
        t = lax.rem(lane + d, lanes)
        pay_copy(t, lane).wait_send()
        pay_copy(t, t).wait_recv()
        return carry

    lax.fori_loop(1, lanes, settle, 0)
    own_pay.wait()
    means_out.wait()


def split3(x):
    high = x.astype(BF16)
    rest = x - high.astype(F32)
    mid = rest.astype(BF16)
    low = (rest - mid.astype(F32)).astype(BF16)
    return high, mid, low


def refine_kernel(
    pseudo, pay_in, means, coarse_in, parent_in, offsets_in, means_ref, out_ref,
    pay, coarse, parent, offsets, factors, norms, load,
):
    loads = [
        pltpu.make_async_copy(source, target, load.at[i])
        for i, (source, target) in enumerate(
            ((pay_in, pay), (coarse_in, coarse), (parent_in, parent), (offsets_in, offsets), (means, means_ref))
        )
    ]
    for part in loads:
        part.start()
    for part in loads[:-1]:
        part.wait()
    sources, _, fragments = pay.shape
    chans = out_ref.shape[0]
    coarse_count = coarse.shape[1]
    fine = out_ref.shape[1]
    select = (
        jnp.broadcast_to(parent[...], (coarse_count, fine))
        == lax.broadcasted_iota(jnp.int32, (coarse_count, fine), 0)
    ).astype(F32)
    cents = jnp.dot(coarse[...], select, precision=HIGH, preferred_element_type=F32) + offsets[...]

    def prepare(s, carry):
        frags = pay[s, :chans, :]
        fh, fm, fl = split3(2.0 * sharpness * frags)
        ones = jnp.full((3 * chans, fragments), -sharpness, BF16)
        factors[s] = jnp.concatenate([fh, fm, fh, fl, fm, fh, ones], axis=0)
        norms[s] = -sharpness * jnp.sum(frags * frags, axis=0, keepdims=True)
        return carry

    lax.fori_loop(0, sources, prepare, 0)

    bunch = 4 if sources % 4 == 0 else 1

    def iterate(step, cents):
        ch, cm, cl = split3(cents)
        sh, sm, sl = split3(cents * cents)
        keys = jnp.concatenate([ch, ch, cm, ch, cm, cl, sh, sm, sl], axis=0)

        def visit(group, total):
            left, high, middle = [], [], []
            for k in range(bunch):
                s = group * bunch + k
                scores = norms[s] + lax.dot_general(
                    keys, factors[s], (((0,), (0,)), ((), ())), preferred_element_type=F32
                )
                top = jnp.max(scores, axis=0, keepdims=True)
                expo = jnp.exp(scores - top)
                scale = pay[s, chans : chans + 1, :] / jnp.sum(expo, axis=0, keepdims=True)
                scale = jnp.broadcast_to(scale, (chans, fragments))
                left.append(jnp.concatenate(split3(jnp.concatenate([pay[s, :chans, :] * scale, scale], axis=0)), axis=0))
                eh = expo.astype(BF16)
                high.append(eh)
                middle.append((expo - eh.astype(F32)).astype(BF16))
            dims = (((1,), (1,)), ((), ()))
            size = 2 * chans
            left = jnp.concatenate(left, axis=1)
            first = lax.dot_general(
                left, jnp.concatenate(high, axis=1), dims, preferred_element_type=F32
            )
            second = lax.dot_general(
                left[: 2 * size], jnp.concatenate(middle, axis=1), dims, preferred_element_type=F32
            )
            return (
                total
                + (first[2 * size :] + second[size:])
                + (first[size : 2 * size] + second[:size])
                + first[:size]
            )

        total = lax.fori_loop(0, sources // bunch, visit, jnp.zeros((2 * chans, fine), F32))
        return (total[:chans] + pseudo * cents) / (total[chans:] + pseudo)

    out_ref[...] = lax.fori_loop(0, ITERS, iterate, cents)
    loads[-1].wait()


def shards(
    slab_image,
    width_taps,
    height_taps,
    depth_taps,
    fragment_ids,
    fragment_owner,
    coarse_centroids,
    parent_map,
    fine_offsets,
):
    chans = width_taps.shape[0]
    depth, rows, cols = fragment_ids.shape
    fragments = fragment_owner.shape[0]
    lanes = lax.axis_size("xy")
    stacks = lax.axis_size("gz")
    padded_rows = rows + TAPS - 1
    slab_depth, height, _ = slab_image.shape
    highs = fragments // LO
    assert highs <= 16
    cap = min(CAP, fragments)
    gathered, means = pl.pallas_call(
        pencil_kernel,
        out_shape=(
            jax.ShapeDtypeStruct((lanes, chans + 8, cap), F32),
            jax.ShapeDtypeStruct((chans, fragments), F32),
        ),
        in_specs=[pl.BlockSpec(memory_space=pltpu.HBM)] * 6,
        out_specs=(pl.BlockSpec(memory_space=pltpu.HBM),) * 2,
        scratch_shapes=[
            pltpu.VMEM((slab_depth, height + 16, cols), F32),
            pltpu.VMEM((stacks, slab_depth * padded_rows, cols), BF16),
            pltpu.VMEM((stacks, slab_depth * padded_rows, cols), BF16),
            pltpu.VMEM((slab_depth * padded_rows, cols), F32),
            pltpu.VMEM((slab_depth * padded_rows, LANE), F32),
            pltpu.VMEM((2, slab_depth * HALF, height), F32),
            pltpu.VMEM((2, stacks, slab_depth * HALF, height), F32),
            pltpu.VMEM((height + 16, LANE), F32),
            pltpu.VMEM((LANE, LANE), F32),
            pltpu.VMEM((2, LANE, 2 * LANE), BF16),
            pltpu.VMEM((depth + 2 * HALF, rows * chans, cols), F32),
            pltpu.VMEM((depth, rows, cols), jnp.int32),
            pltpu.VMEM((cols // LANE, depth, rows, LANE), F32),
            pltpu.VMEM((cols // LANE, depth, rows, LANE), F32),
            pltpu.VMEM((cols // LANE, depth, rows, LANE), F32),
            pltpu.VMEM((cols // LANE, depth, rows, LANE), F32),
            pltpu.VMEM((highs * chans, LO), F32),
            pltpu.VMEM((LO // FEW * highs, FEW), F32),
            pltpu.VMEM((TAPS, chans), F32),
            pltpu.VMEM((TAPS, chans), F32),
            pltpu.VMEM((TAPS, chans), F32),
            pltpu.VMEM((highs, LANE), jnp.int32),
            pltpu.VMEM((lanes * highs, LANE), F32),
            pltpu.VMEM((lanes, chans + 8, cap), F32),
            pltpu.VMEM((chans, fragments), F32),
            pltpu.SemaphoreType.DMA((6,)),
            pltpu.SemaphoreType.DMA((stacks,)),
            pltpu.SemaphoreType.DMA((stacks,)),
            pltpu.SemaphoreType.DMA((2, stacks)),
            pltpu.SemaphoreType.DMA((2, stacks)),
            pltpu.SemaphoreType.DMA((lanes,)),
            pltpu.SemaphoreType.DMA((lanes,)),
        ],
        compiler_params=pltpu.CompilerParams(
            collective_id=0, has_side_effects=True, vmem_limit_bytes=60 << 20
        ),
        name="pencil",
    )(slab_image, fragment_ids, width_taps.T, height_taps.T, depth_taps.T, fragment_owner.reshape(highs, LANE))
    fine = fine_offsets.shape[1]
    pseudo = float(fragment_ids.size // fine)
    return pl.pallas_call(
        functools.partial(refine_kernel, pseudo),
        out_shape=(
            jax.ShapeDtypeStruct((chans, fragments), F32),
            jax.ShapeDtypeStruct((chans, fine), F32),
        ),
        in_specs=[pl.BlockSpec(memory_space=pltpu.HBM)] * 5,
        out_specs=(pl.BlockSpec(memory_space=pltpu.HBM), pl.BlockSpec(memory_space=pltpu.VMEM)),
        scratch_shapes=[
            pltpu.VMEM((lanes, chans + 8, cap), F32),
            pltpu.VMEM(coarse_centroids.shape, F32),
            pltpu.VMEM((1, fine), jnp.int32),
            pltpu.VMEM((chans, fine), F32),
            pltpu.VMEM((lanes, 9 * chans, cap), BF16),
            pltpu.VMEM((lanes, 1, cap), F32),
            pltpu.SemaphoreType.DMA((5,)),
        ],
        compiler_params=pltpu.CompilerParams(vmem_limit_bytes=60 << 20),
        name="refine",
    )(gathered, means, coarse_centroids, parent_map.reshape(1, fine), fine_offsets)


def solution(mesh):
    placed = (
        P("gz", None, "xy"),
        P(),
        P(),
        P(),
        P(None, "gz", "xy"),
        P(("gz", "xy"), None),
        P(None, ("gz", "xy")),
        P(("gz", "xy")),
        P(None, ("gz", "xy")),
    )
    return jax.shard_map(
        shards,
        mesh=mesh,
        in_specs=placed,
        out_specs=(P(None, ("gz", "xy")), P(None, ("gz", "xy"))),
        check_vma=False,
    )
```
